32 devices in a mesh: dp: 8 (over z, x), row: 2 (over y), col: 2 (over core).
Axes of the slice: x: 2, y: 2, z: 4, core: 2. Of those that a mesh axis runs over, the one named last changes fastest.
Arguments:
- tokens: bfloat16 [4096, 768], P('dp', 'col'), may hold values from -3 to 3
- cond: bfloat16 [16, 768], P('dp', 'col'), may hold values from -2.5 to 2.5
- w_ada: bfloat16 [768, 4608], P('row', 'col'), may hold values from -0.21875 to 0.21875
- b_ada: float32 [4608], P('col'), may hold values from -0.75 to 0.75
- query_key_value_weight: bfloat16 [768, 2304], P('row', 'col'), may hold values from -0.21875 to 0.21875
- b_qv: float32 [2, 768], P(None, 'col'), may hold values from -0.75 to 0.75
- projection_weight: bfloat16 [768, 768], P('row', 'col'), may hold values from -0.875 to 0.875
- projection_bias: float32 [768], P('col'), may hold values from -0.75 to 0.75
- w_fc1: bfloat16 [768, 3072], P('row', 'col'), may hold values from -0.21875 to 0.21875
- b_fc1: float32 [3072], P('col'), may hold values from -0.75 to 0.75
- w_fc2: bfloat16 [3072, 768], P('row', 'col'), may hold values from -0.21875 to 0.21875
- b_fc2: float32 [768], P('col'), may hold values from -0.75 to 0.75
- cotangent: bfloat16 [4096, 768], P('dp', 'col'), may hold values from -3 to 3
Outputs:
- output: bfloat16 [4096, 768], P('dp', 'col')
- token_gradient: bfloat16 [4096, 768], P('dp', 'col')
- grad_cond: bfloat16 [16, 768], P('dp', 'col')
- grad_w_ada: float32 [2, 384, 4608], P('row', 'dp', 'col')
- grad_b_ada: float32 [4608], P('col')
- grad_w_qkv: float32 [2, 384, 2304], P('row', 'dp', 'col')
- grad_b_qv: float32 [2, 768], P(None, 'col')
- grad_w_proj: float32 [2, 384, 768], P('row', 'dp', 'col')
- grad_b_proj: float32 [768], P('col')
- grad_w_fc1: float32 [2, 384, 3072], P('row', 'dp', 'col')
- grad_b_fc1: float32 [3072], P('col')
- grad_w_fc2: float32 [2, 1536, 768], P('row', 'dp', 'col')
- grad_b_fc2: float32 [768], P('col')
The draws below stay inside these ranges and needn't reach their ends.
All inputs are finite; a program needn't handle non-finite values.
Results may differ from the reference program's by a relative error of at most 0.018.
Values may be sent and summed in bfloat16 or wider, within the bound.
No kernel may reach another device: no remote copies, remote signals or barrier semaphores. Data moves between devices by JAX's collectives and lax.ppermute only.
A program may use at most 128 MiB of HBM per device.

```python
from functools import partial
import jax
import jax.numpy as jnp
from jax import lax

MODEL_WIDTH = 768
ATTENTION_HEADS = 12
HEAD_SIZE = 64
FF = 3072
LATENT_TOKENS = 256
LAT_DEV = 2
LATENTS = 16
TOKENS = 4096
N_DP = 8
N_ROW = 2
N_COL = 2


def block_levels(own_key, shape, cuts, smallest, largest):
    def one(position, blocks):
        steps = jax.random.uniform(jax.random.fold_in(jax.random.fold_in(own_key, 6), position), (blocks,), jnp.float32, smallest / len(cuts), largest / len(cuts))
        return jnp.repeat(jnp.exp(steps), shape[position] // blocks).reshape((-1,) + (1,) * (len(shape) - position - 1))

    level = one(*cuts[0])
    for cut in cuts[1:]:
        level = level * one(*cut)
    return level


def bell_draw(key, dims, deviation, most, shards=(), dtype=jnp.bfloat16):
    array = deviation * jax.random.normal(key, dims, jnp.float32)
    if shards:
        array = array * block_levels(key, dims, shards, -0.22, 0.18)
    return jnp.clip(array, -most, most).astype(dtype)


def setup_inputs(seed: int = 0) -> dict:
    key_of = jax.random.split(jax.random.key(seed), 14)
    return {
        "tokens": bell_draw(key_of[0], (TOKENS, MODEL_WIDTH), 1.0, 3.0, ((0, 8), (1, 2))),
        "cond": bell_draw(key_of[1], (LATENTS, MODEL_WIDTH), 1.0, 2.5, ((0, 8), (1, 2))),
        "w_ada": bell_draw(key_of[2], (MODEL_WIDTH, 6 * MODEL_WIDTH), MODEL_WIDTH ** -0.5, 0.21875, ((0, 2), (1, 2))),
        "b_ada": bell_draw(key_of[3], (6 * MODEL_WIDTH,), 0.3, 0.75, ((0, 2),), jnp.float32),
        "query_key_value_weight": bell_draw(key_of[4], (MODEL_WIDTH, 3 * MODEL_WIDTH), MODEL_WIDTH ** -0.5, 0.21875, ((0, 2), (1, 2))),
        "b_qv": bell_draw(key_of[5], (2, MODEL_WIDTH), 0.3, 0.75, ((1, 2),), jnp.float32),
        "projection_weight": bell_draw(key_of[6], (MODEL_WIDTH, MODEL_WIDTH), (MODEL_WIDTH // 16) ** -0.5, 0.875, ((0, 2), (1, 2))),
        "projection_bias": bell_draw(key_of[7], (MODEL_WIDTH,), 0.3, 0.75, ((0, 2),), jnp.float32),
        "w_fc1": bell_draw(key_of[8], (MODEL_WIDTH, FF), MODEL_WIDTH ** -0.5, 0.21875, ((0, 2), (1, 2))),
        "b_fc1": bell_draw(key_of[9], (FF,), 0.3, 0.75, ((0, 2),), jnp.float32),
        "w_fc2": bell_draw(key_of[10], (FF, MODEL_WIDTH), (FF // 4) ** -0.5, 0.21875, ((0, 2), (1, 2))),
        "b_fc2": bell_draw(key_of[11], (MODEL_WIDTH,), 0.3, 0.75, ((0, 2),), jnp.float32),
        "cotangent": bell_draw(key_of[12], (TOKENS, MODEL_WIDTH), 1.0, 3.0, ((0, 8), (1, 2))),
    }


norm_eps = 1e-06
gelu_coef = 0.7978845608028654

def narrowed(values):
    return values.astype(jnp.bfloat16)

def product_forward(active, weight):
    return jnp.dot(active, weight, preferred_element_type=jnp.float32)

def product_backward(grads, weight):
    return jnp.dot(grads, weight.T, preferred_element_type=jnp.float32)

def weight_gradient(active, grads):
    return jnp.dot(active.T, grads, preferred_element_type=jnp.float32)

def norm_rowwise(values):
    mean = lax.optimization_barrier(jnp.mean(values, axis=-1, keepdims=True))
    msq = lax.optimization_barrier(jnp.mean(values * values, axis=-1, keepdims=True))
    rstd = lax.rsqrt(msq - mean * mean + norm_eps)
    return ((values - mean) * rstd, rstd)

def norm_backward(dnorm, normed, rstd):
    first = lax.optimization_barrier(jnp.mean(dnorm, axis=-1, keepdims=True))
    second = lax.optimization_barrier(jnp.mean(dnorm * normed, axis=-1, keepdims=True))
    return rstd * (dnorm - first - normed * second)

def gelu_pair(upper):
    inner = jnp.tanh(gelu_coef * (upper + 0.044715 * upper * upper * upper))
    value = 0.5 * upper * (1.0 + inner)
    slope = 0.5 * (1.0 + inner) + 0.5 * upper * (1.0 - inner * inner) * gelu_coef * (1.0 + 3.0 * 0.044715 * upper * upper)
    return (value, slope)

def attention_scores(query, key):
    scale = query.shape[-1] ** (-0.5)
    return jnp.einsum('bqhd,bkhd->bhqk', query.astype(jnp.float32), key.astype(jnp.float32)) * scale

def one_shard(weights, carry, inputs):
    w_ada_all, b_ada_all, query_key_value_weight_stack, b_qv_all, projection_weight_stack, projection_bias_stack, w_fc1_all, b_fc1_all, w_fc2_all, b_fc2_all = weights
    tok_block, cond_block, cot_block = inputs
    latent_tokens = cond_block.shape[0]
    halved_width = MODEL_WIDTH // N_COL
    shard_heads = ATTENTION_HEADS // N_COL
    scale = HEAD_SIZE ** (-0.5)
    cond32 = cond_block.astype(jnp.float32)
    silu_cond = narrowed(jax.nn.silu(cond32))
    modulation = product_forward(silu_cond, w_ada_all) + b_ada_all
    modulation = modulation.reshape(latent_tokens, N_COL, 6, halved_width).transpose(0, 2, 1, 3).reshape(latent_tokens, 6, MODEL_WIDTH)
    device_roles = [modulation[:, index][:, None, :] for index in range(6)]
    attention_offset, attention_scale, attention_gate, perceptron_offset, perceptron_scale, perceptron_gate = device_roles
    input_float32 = tok_block.astype(jnp.float32).reshape(latent_tokens, LATENT_TOKENS, MODEL_WIDTH)
    attention_norm, attention_inverse_deviation = norm_rowwise(input_float32)
    attention_hidden = narrowed(attention_norm * (1.0 + attention_scale) + attention_offset).reshape(latent_tokens * LATENT_TOKENS, MODEL_WIDTH)
    query_key_value = product_forward(attention_hidden, query_key_value_weight_stack).reshape(latent_tokens, LATENT_TOKENS, N_COL, 3, shard_heads, HEAD_SIZE)
    bias_pair = b_qv_all.reshape(2, ATTENTION_HEADS, HEAD_SIZE)
    query = narrowed(query_key_value[:, :, :, 0].reshape(latent_tokens, LATENT_TOKENS, ATTENTION_HEADS, HEAD_SIZE) + bias_pair[0])
    key = narrowed(query_key_value[:, :, :, 1].reshape(latent_tokens, LATENT_TOKENS, ATTENTION_HEADS, HEAD_SIZE))
    value = narrowed(query_key_value[:, :, :, 2].reshape(latent_tokens, LATENT_TOKENS, ATTENTION_HEADS, HEAD_SIZE) + bias_pair[1])
    scores = attention_scores(query, key)
    top = lax.optimization_barrier(jnp.max(scores, axis=-1, keepdims=True))
    lse = top + jnp.log(lax.optimization_barrier(jnp.sum(jnp.exp(scores - top), axis=-1, keepdims=True)))
    probs_b = narrowed(jnp.exp(scores - lse))
    attention_output = narrowed(jnp.einsum('bhqk,bkhd->bqhd', probs_b.astype(jnp.float32), value.astype(jnp.float32))).reshape(latent_tokens * LATENT_TOKENS, MODEL_WIDTH)
    attention_branch = (product_forward(attention_output, projection_weight_stack) + projection_bias_stack).reshape(latent_tokens, LATENT_TOKENS, MODEL_WIDTH)
    residual_state = input_float32 + attention_gate * attention_branch
    norm_mlp, rstd_mlp = norm_rowwise(residual_state)
    hidden_mlp = narrowed(norm_mlp * (1.0 + perceptron_scale) + perceptron_offset).reshape(latent_tokens * LATENT_TOKENS, MODEL_WIDTH)
    upper = product_forward(hidden_mlp, w_fc1_all) + b_fc1_all
    gelu_value, gelu_slope = gelu_pair(upper)
    activated = narrowed(gelu_value)
    branch_mlp = (product_forward(activated, w_fc2_all) + b_fc2_all).reshape(latent_tokens, LATENT_TOKENS, MODEL_WIDTH)
    output = narrowed(residual_state + perceptron_gate * branch_mlp).reshape(latent_tokens * LATENT_TOKENS, MODEL_WIDTH)
    grad_out = cot_block.astype(jnp.float32).reshape(latent_tokens, LATENT_TOKENS, MODEL_WIDTH)
    perceptron_gate_gradient = lax.optimization_barrier(jnp.sum(grad_out * branch_mlp, axis=1))
    perceptron_branch_gradient = (grad_out * perceptron_gate).reshape(latent_tokens * LATENT_TOKENS, MODEL_WIDTH)
    d_branch_mlp_b = narrowed(perceptron_branch_gradient)
    down_weight_gradient = weight_gradient(activated, d_branch_mlp_b)
    expanded_gradient = product_backward(d_branch_mlp_b, w_fc2_all) * gelu_slope
    d_upper_b = narrowed(expanded_gradient)
    up_weight_gradient = weight_gradient(hidden_mlp, d_upper_b)
    d_hidden_mlp = product_backward(d_upper_b, w_fc1_all).reshape(latent_tokens, LATENT_TOKENS, MODEL_WIDTH)
    perceptron_offset_gradient = lax.optimization_barrier(jnp.sum(d_hidden_mlp, axis=1))
    perceptron_scale_gradient = lax.optimization_barrier(jnp.sum(d_hidden_mlp * norm_mlp, axis=1))
    residual_gradient = grad_out + norm_backward(d_hidden_mlp * (1.0 + perceptron_scale), norm_mlp, rstd_mlp)
    attention_gate_gradient = lax.optimization_barrier(jnp.sum(residual_gradient * attention_branch, axis=1))
    attention_branch_gradient = (residual_gradient * attention_gate).reshape(latent_tokens * LATENT_TOKENS, MODEL_WIDTH)
    attention_branch_gradient_bias = narrowed(attention_branch_gradient)
    projection_weight_gradient = weight_gradient(attention_output, attention_branch_gradient_bias)
    attention_output_gradient = narrowed(product_backward(attention_branch_gradient_bias, projection_weight_stack)).reshape(latent_tokens, LATENT_TOKENS, ATTENTION_HEADS, HEAD_SIZE)
    probs = jnp.exp(attention_scores(query, key) - lse)
    probs_b2 = narrowed(probs).astype(jnp.float32)
    d_att32 = attention_output_gradient.astype(jnp.float32)
    d_value = jnp.einsum('bhqk,bqhd->bkhd', probs_b2, d_att32)
    d_probs = jnp.einsum('bqhd,bkhd->bhqk', d_att32, value.astype(jnp.float32))
    d_scores = probs * (d_probs - lax.optimization_barrier(jnp.sum(probs * d_probs, axis=-1, keepdims=True)))
    d_scores_b = narrowed(d_scores).astype(jnp.float32)
    d_query = jnp.einsum('bhqk,bkhd->bqhd', d_scores_b, key.astype(jnp.float32)) * scale
    d_key = jnp.einsum('bhqk,bqhd->bkhd', d_scores_b, query.astype(jnp.float32)) * scale
    query_value_bias_gradient = jnp.stack([lax.optimization_barrier(jnp.sum(d_query, axis=(0, 1))).reshape(MODEL_WIDTH), lax.optimization_barrier(jnp.sum(d_value, axis=(0, 1))).reshape(MODEL_WIDTH)])
    d_qkv = jnp.stack([d_query, d_key, d_value], axis=2).reshape(latent_tokens, LATENT_TOKENS, 3, N_COL, shard_heads, HEAD_SIZE)
    query_key_value_gradient = narrowed(d_qkv.transpose(0, 1, 3, 2, 4, 5).reshape(latent_tokens * LATENT_TOKENS, 3 * MODEL_WIDTH))
    query_key_value_weight_gradient = weight_gradient(attention_hidden, query_key_value_gradient)
    attention_hidden_gradient = product_backward(query_key_value_gradient, query_key_value_weight_stack).reshape(latent_tokens, LATENT_TOKENS, MODEL_WIDTH)
    attention_offset_gradient = lax.optimization_barrier(jnp.sum(attention_hidden_gradient, axis=1))
    attention_scale_gradient = lax.optimization_barrier(jnp.sum(attention_hidden_gradient * attention_norm, axis=1))
    token_gradient = narrowed(residual_gradient + norm_backward(attention_hidden_gradient * (1.0 + attention_scale), attention_norm, attention_inverse_deviation)).reshape(latent_tokens * LATENT_TOKENS, MODEL_WIDTH)
    modulation_gradient = jnp.stack([attention_offset_gradient, attention_scale_gradient, attention_gate_gradient, perceptron_offset_gradient, perceptron_scale_gradient, perceptron_gate_gradient], axis=1)
    modulation_gradient = modulation_gradient.reshape(latent_tokens, 6, N_COL, halved_width).transpose(0, 2, 1, 3).reshape(latent_tokens, 6 * MODEL_WIDTH)
    d_modulation_b = narrowed(modulation_gradient)
    modulation_weight_gradient = weight_gradient(silu_cond, d_modulation_b)
    sigmoid_cond = jax.nn.sigmoid(cond32)
    grad_cond = narrowed(product_backward(d_modulation_b, w_ada_all) * sigmoid_cond * (1.0 + cond32 * (1.0 - sigmoid_cond)))
    summands = (modulation_weight_gradient, lax.optimization_barrier(jnp.sum(modulation_gradient, axis=0)), query_key_value_weight_gradient, query_value_bias_gradient, projection_weight_gradient, lax.optimization_barrier(jnp.sum(attention_branch_gradient, axis=0)), up_weight_gradient, lax.optimization_barrier(jnp.sum(expanded_gradient, axis=0)), down_weight_gradient, lax.optimization_barrier(jnp.sum(perceptron_branch_gradient, axis=0)))
    carry = tuple((total + term for total, term in zip(carry, summands)))
    return (carry, (output, token_gradient, grad_cond))

def reference(tokens, cond, w_ada, b_ada, query_key_value_weight, b_qv, projection_weight, projection_bias, w_fc1, b_fc1, w_fc2, b_fc2, cotangent):
    weights = (w_ada, b_ada, query_key_value_weight, b_qv, projection_weight, projection_bias, w_fc1, b_fc1, w_fc2, b_fc2)
    step = partial(one_shard, weights)
    zeros = tuple((jnp.zeros(item.shape, jnp.float32) for item in weights))
    groups = (tokens.reshape(N_DP, LAT_DEV * LATENT_TOKENS, MODEL_WIDTH), cond.reshape(N_DP, LAT_DEV, MODEL_WIDTH), cotangent.reshape(N_DP, LAT_DEV * LATENT_TOKENS, MODEL_WIDTH))
    totals, stacked = lax.scan(step, zeros, groups)
    output = stacked[0].reshape(TOKENS, MODEL_WIDTH)
    token_gradient = stacked[1].reshape(TOKENS, MODEL_WIDTH)
    grad_cond = stacked[2].reshape(LATENTS, MODEL_WIDTH)
    modulation_weight_gradient, d_ada, query_key_value_weight_gradient, d_qv, projection_weight_gradient, d_proj, up_weight_gradient, d_fc1, down_weight_gradient, d_fc2 = totals
    return (output, token_gradient, grad_cond, modulation_weight_gradient.reshape(N_ROW, MODEL_WIDTH // N_ROW, 6 * MODEL_WIDTH), d_ada, query_key_value_weight_gradient.reshape(N_ROW, MODEL_WIDTH // N_ROW, 3 * MODEL_WIDTH), d_qv, projection_weight_gradient.reshape(N_ROW, MODEL_WIDTH // N_ROW, MODEL_WIDTH), d_proj, up_weight_gradient.reshape(N_ROW, MODEL_WIDTH // N_ROW, FF), d_fc1, down_weight_gradient.reshape(N_ROW, FF // N_ROW, MODEL_WIDTH), d_fc2)
```

```python
import jax
import jax.numpy as jnp
from jax import lax
from jax.sharding import PartitionSpec as P

HEAD_SIZE = 64
NORM_EPS = 1e-06
GELU_COEF = 0.7978845608028654
F32 = jnp.float32
BF16 = jnp.bfloat16


def narrowed(values):
    return values.astype(BF16)


def dot(a, b):
    return jnp.dot(a, b, preferred_element_type=F32)


def dot_nt(a, b):
    return lax.dot_general(a, b, (((1,), (1,)), ((), ())), preferred_element_type=F32)


def dot_tn(a, b):
    return lax.dot_general(a, b, (((0,), (0,)), ((), ())), preferred_element_type=F32)


def col_swap(x):
    return lax.ppermute(x, "col", [(0, 1), (1, 0)])


def row_swap(x):
    return lax.ppermute(x, "row", [(0, 1), (1, 0)])


def cross_swap(x):
    return lax.ppermute(x, ("row", "col"), [(0, 3), (1, 2), (2, 1), (3, 0)])


def bit_swap(x, bit):
    size = lax.axis_size("dp")
    return lax.ppermute(x, "dp", [(i, i ^ bit) for i in range(size)])


SECOND = [(1, 0), (2, 3), (3, 1), (0, 2)]
FIRST = [(2, 1), (1, 2), (0, 0), (3, 3)]


def inverse(pairs):
    return [(b, a) for a, b in pairs]


def gelu_pair(upper):
    inner = jnp.tanh(GELU_COEF * (upper + 0.044715 * upper * upper * upper))
    value = 0.5 * upper * (1.0 + inner)
    slope = 0.5 * (1.0 + inner) + 0.5 * upper * (1.0 - inner * inner) * GELU_COEF * (
        1.0 + 3.0 * 0.044715 * upper * upper
    )
    return value, slope


def norm_rowwise(values):
    mean = jnp.mean(values, axis=-1, keepdims=True)
    msq = jnp.mean(values * values, axis=-1, keepdims=True)
    rstd = lax.rsqrt(msq - mean * mean + NORM_EPS)
    return (values - mean) * rstd, rstd


def norm_backward(dnorm, normed, rstd):
    first = jnp.mean(dnorm, axis=-1, keepdims=True)
    second = jnp.mean(dnorm * normed, axis=-1, keepdims=True)
    return rstd * (dnorm - first - normed * second)


def halve_bit(block, bit, position):
    mine = (lax.axis_index("dp") // bit) % 2
    keep = lax.dynamic_index_in_dim(block, mine, position, keepdims=False)
    send = lax.dynamic_index_in_dim(block, 1 - mine, position, keepdims=False)
    return keep, bit_swap(send, bit)


def add(a, b):
    return narrowed(a.astype(F32) + b.astype(F32))


def dp_bits():
    size = lax.axis_size("dp")
    bits = []
    bit = 1
    while bit < size:
        bits.append(bit)
        bit *= 2
    return bits


def split_dp(block):
    bits = dp_bits()
    lead = block.shape[:-2]
    rows, cols = block.shape[-2:]
    return block.reshape(lead + (2,) * len(bits) + (rows // lax.axis_size("dp"), cols))


def scatter_bits(view, bits, last=True):
    for i, bit in enumerate(bits):
        keep, got = halve_bit(view, bit, view.ndim - 3)
        if last and i == len(bits) - 1:
            view = keep.astype(F32) + got.astype(F32)
        else:
            view = add(keep, got)
    return view


def body(tokens, cond, w_ada, b_ada, w_qkv, b_qv, w_proj, b_proj, w_fc1, b_fc1, w_fc2, b_fc2, cotangent):
    r = lax.axis_index("row")
    c = lax.axis_index("col")
    diag = r == c
    half = tokens.shape[1]
    seq = tokens.shape[0] // 2
    heads = w_qkv.shape[1] // (3 * HEAD_SIZE)
    scale = HEAD_SIZE ** (-0.5)

    def own_tokens(x):
        return lax.dynamic_slice_in_dim(x, r * seq, seq, 0)

    def ordered(mine, other):
        return jnp.concatenate(
            [jnp.where(diag, mine, other), jnp.where(diag, other, mine)], axis=-1
        )

    def block_c(x):
        return jnp.where(diag, x[..., :half], x[..., half:])

    def block_other(x):
        return jnp.where(diag, x[..., half:], x[..., :half])

    def both_rows(x):
        other = row_swap(x)
        return jnp.concatenate(
            [jnp.where(r == 0, x, other), jnp.where(r == 0, other, x)], axis=0
        )

    cond_other = col_swap(cond)
    tok_mine = own_tokens(tokens)
    tok_other = col_swap(tok_mine)
    wq2 = row_swap(w_qkv)
    wp_b = lax.ppermute(w_proj, ("row", "col"), SECOND)
    wp_a = lax.ppermute(w_proj, ("row", "col"), FIRST)
    w12 = row_swap(w_fc1)
    w2_b = lax.ppermute(w_fc2, ("row", "col"), SECOND)
    w2_a = lax.ppermute(w_fc2, ("row", "col"), FIRST)
    cot_mine = own_tokens(cotangent)
    cot_other = col_swap(cot_mine)

    cond_r = jnp.where(diag, cond, cond_other).astype(F32)
    silu_r = narrowed(jax.nn.silu(cond_r))
    part = dot(silu_r, w_ada)
    part_mine = lax.dynamic_index_in_dim(part, r, 0, keepdims=False)
    part_away = lax.dynamic_index_in_dim(part, 1 - r, 0, keepdims=False)
    biases = jnp.concatenate([part_mine + b_ada, b_proj, b_fc2])
    got_col = col_swap(biases)
    got_row = row_swap(part_away)
    got_cross = cross_swap(part_away)
    n_ada = b_ada.shape[0]
    mod_c = (biases[:n_ada] + got_row).reshape(6, half)
    mod_o = (got_col[:n_ada] + got_cross).reshape(6, half)
    mod = ordered(mod_c, mod_o)
    shift1, scale1, gate1, shift2, scale2, gate2 = [mod[i : i + 1] for i in range(6)]
    bias_p = ordered(b_proj, got_col[n_ada : n_ada + half])

    x = ordered(tok_mine, tok_other).astype(F32)
    n1, rstd1 = norm_rowwise(x)
    h1 = narrowed(n1 * (1.0 + scale1) + shift1)
    qkv = dot(h1[:, :half], w_qkv) + dot(h1[:, half:], wq2)
    q = narrowed(qkv[:, :half] + b_qv[0]).reshape(seq, heads, HEAD_SIZE)
    k = narrowed(qkv[:, half : 2 * half]).reshape(seq, heads, HEAD_SIZE)
    v = narrowed(qkv[:, 2 * half :] + b_qv[1]).reshape(seq, heads, HEAD_SIZE)
    scores = jnp.einsum("qhd,khd->hqk", q, k, preferred_element_type=F32) * scale
    top = jnp.max(scores, axis=-1, keepdims=True)
    lse = top + jnp.log(jnp.sum(jnp.exp(scores - top), axis=-1, keepdims=True))
    probs = jnp.exp(scores - lse)
    probs_b = narrowed(probs)
    att = narrowed(jnp.einsum("hqk,khd->qhd", probs_b, v, preferred_element_type=F32)).reshape(seq, half)
    bp = jnp.concatenate([dot(att, wp_a), dot(att, wp_b)], axis=-1)
    branch1 = bp + col_swap(narrowed(bp)).astype(F32) + bias_p
    mid = x + gate1 * branch1

    n2, rstd2 = norm_rowwise(mid)
    h2 = narrowed(n2 * (1.0 + scale2) + shift2)
    upper = dot(h2[:, :half], w_fc1) + dot(h2[:, half:], w12) + b_fc1
    value, slope = gelu_pair(upper)
    act = narrowed(value)
    down = jnp.concatenate([dot(act, w2_a), dot(act, w2_b)], axis=-1)
    branch2 = block_c(down) + col_swap(narrowed(block_other(down))).astype(F32) + b_fc2
    out_c = narrowed(block_c(mid) + mod_c[5] * branch2)
    output = both_rows(out_c)

    g_c = cot_mine.astype(F32)
    g = ordered(cot_mine, cot_other).astype(F32)
    d_gate2 = jnp.sum(g_c * branch2, axis=0)
    d_branch2 = g * gate2
    gb_fc2 = jnp.sum(g_c * mod_c[5], axis=0)
    d_branch2_b = narrowed(d_branch2)
    d_upper = (dot_nt(d_branch2_b[:, :half], w2_a) + dot_nt(d_branch2_b[:, half:], w2_b)) * slope
    gb_fc1 = jnp.sum(d_upper, axis=0)
    d_upper_b = narrowed(d_upper)
    g_fc2 = narrowed(dot_tn(act, d_branch2_b))
    d_h2 = jnp.concatenate([dot_nt(d_upper_b, w_fc1), dot_nt(d_upper_b, w12)], axis=-1)
    d_h2 = d_h2 + col_swap(narrowed(d_h2)).astype(F32)
    g_fc1 = narrowed(dot_tn(h2, d_upper_b))
    d_shift2 = jnp.sum(d_h2, axis=0)
    d_scale2 = jnp.sum(d_h2 * n2, axis=0)
    d_mid = g + norm_backward(d_h2 * (1.0 + scale2), n2, rstd2)

    d_gate1 = jnp.sum(d_mid * branch1, axis=0)
    d_branch1 = d_mid * gate1
    gb_proj = jnp.sum(d_branch1, axis=0)
    d_branch1_b = narrowed(d_branch1)
    d_att = narrowed(dot_nt(d_branch1_b[:, :half], wp_a) + dot_nt(d_branch1_b[:, half:], wp_b))
    d_att = d_att.reshape(seq, heads, HEAD_SIZE)
    g_proj = narrowed(dot_tn(att, d_branch1_b))
    d_v = jnp.einsum("hqk,qhd->khd", probs_b, d_att, preferred_element_type=F32)
    d_probs = jnp.einsum("qhd,khd->hqk", d_att, v, preferred_element_type=F32)
    d_scores = probs * (d_probs - jnp.sum(probs * d_probs, axis=-1, keepdims=True))
    d_scores_b = narrowed(d_scores)
    d_q = jnp.einsum("hqk,khd->qhd", d_scores_b, k, preferred_element_type=F32) * scale
    d_k = jnp.einsum("hqk,qhd->khd", d_scores_b, q, preferred_element_type=F32) * scale
    d_q, d_k, d_v = (t.reshape(seq, half) for t in (d_q, d_k, d_v))
    gb_q = jnp.sum(d_q, axis=0)
    gb_v = jnp.sum(d_v, axis=0)
    d_qkv = narrowed(jnp.concatenate([d_q, d_k, d_v], axis=-1))
    g_qkv = narrowed(dot_tn(h1, d_qkv))
    d_h1 = jnp.concatenate([dot_nt(d_qkv, w_qkv), dot_nt(d_qkv, wq2)], axis=-1)
    d_h1 = d_h1 + col_swap(narrowed(d_h1)).astype(F32)
    d_shift1 = jnp.sum(d_h1, axis=0)
    d_scale1 = jnp.sum(d_h1 * n1, axis=0)
    tok_grad = narrowed(block_c(d_mid + norm_backward(d_h1 * (1.0 + scale1), n1, rstd1)))
    token_gradient = both_rows(tok_grad)

    bits = dp_bits()

    def column_form(full):
        away = row_swap(full[half:])
        return scatter_bits(split_dp(add(full[:half], away)), bits)

    def row_form(full):
        a = lax.ppermute(full[:, half:], ("row", "col"), inverse(SECOND))
        b = lax.ppermute(full[:, :half], ("row", "col"), inverse(FIRST))
        return scatter_bits(split_dp(add(a, b)), bits)

    out_fc2 = row_form(g_fc2)[None]
    out_fc1 = column_form(g_fc1)[None]
    out_proj = row_form(g_proj)[None]
    out_qkv = column_form(g_qkv)[None]

    d_mod = jnp.stack(
        [block_c(d_shift1), block_c(d_scale1), block_c(d_gate1), block_c(d_shift2), block_c(d_scale2), d_gate2]
    )
    latent = d_mod[None]
    sums = jnp.concatenate(
        [gb_q[None], gb_v[None], block_c(gb_proj)[None], gb_fc1.reshape(-1, half), gb_fc2[None]]
    )
    got_latent, got_sums = row_swap((latent, sums))
    sums = sums + got_sums
    pair = jnp.concatenate([jnp.where(r == 0, latent, got_latent), jnp.where(r == 0, got_latent, latent)])
    d_mod_pair = narrowed(pair.reshape(2, 6 * half))
    pair = jnp.concatenate([pair, silu_r.astype(F32)[:, None]], axis=1)
    d_cond = dot_nt(d_mod_pair, w_ada)
    d_cond = d_cond + col_swap(d_cond)
    d_cond = jnp.where(diag, d_cond, row_swap(d_cond))
    cond32 = cond.astype(F32)
    sig = jax.nn.sigmoid(cond32)
    grad_cond = narrowed(d_cond * sig * (1.0 + cond32 * (1.0 - sig)))
    for bit in bits:
        got_pair, got_sums = bit_swap((pair, sums), bit)
        pair = jnp.concatenate([pair, got_pair])
        sums = sums + got_sums
    n_all = pair.shape[0]
    d_mod_all = pair[:, :6].reshape(n_all, 6 * half)
    rows = half // lax.axis_size("dp")
    silu_rows = narrowed(lax.dynamic_slice_in_dim(pair[:, 6], lax.axis_index("dp") * rows, rows, 1))
    out_ada = dot_tn(silu_rows, narrowed(d_mod_all))[None]
    out_b_ada = jnp.sum(d_mod_all, axis=0)
    out_b_qv = sums[:2]
    out_b_proj = sums[2]
    out_b_fc1 = sums[3:-1].reshape(-1)
    out_b_fc2 = sums[-1]
    return (
        output, token_gradient, grad_cond, out_ada, out_b_ada, out_qkv, out_b_qv,
        out_proj, out_b_proj, out_fc1, out_b_fc1, out_fc2, out_b_fc2,
    )


def solution(mesh):
    in_specs = (
        P("dp", "col"), P("dp", "col"), P("row", "col"), P("col"), P("row", "col"), P(None, "col"),
        P("row", "col"), P("col"), P("row", "col"), P("col"), P("row", "col"), P("col"), P("dp", "col"),
    )
    out_specs = (
        P("dp", "col"), P("dp", "col"), P("dp", "col"), P("row", "dp", "col"), P("col"),
        P("row", "dp", "col"), P(None, "col"), P("row", "dp", "col"), P("col"), P("row", "dp", "col"),
        P("col"), P("row", "dp", "col"), P("col"),
    )
    return jax.shard_map(body, mesh=mesh, in_specs=in_specs, out_specs=out_specs, check_vma=False)
```

```python
import jax
import jax.numpy as jnp
from jax import lax
from jax.experimental import pallas as pl
from jax.experimental.pallas import tpu as pltpu
from jax.sharding import PartitionSpec as P

HEAD_SIZE = 64
NORM_EPS = 1e-06
GELU_COEF = 0.7978845608028654
F32 = jnp.float32
BF16 = jnp.bfloat16


def narrowed(values):
    return values.astype(BF16)


def dot(a, b):
    return jnp.dot(a, b, preferred_element_type=F32)


def dot_nt(a, b):
    return lax.dot_general(a, b, (((1,), (1,)), ((), ())), preferred_element_type=F32)


def dot_tn(a, b):
    return lax.dot_general(a, b, (((0,), (0,)), ((), ())), preferred_element_type=F32)


def col_swap(x):
    return lax.ppermute(x, "col", [(0, 1), (1, 0)])


def row_swap(x):
    return lax.ppermute(x, "row", [(0, 1), (1, 0)])


def cross_swap(x):
    return lax.ppermute(x, ("row", "col"), [(0, 3), (1, 2), (2, 1), (3, 0)])


def bit_swap(x, bit):
    size = lax.axis_size("dp")
    return lax.ppermute(x, "dp", [(i, i ^ bit) for i in range(size)])


SECOND = [(1, 0), (2, 3), (3, 1), (0, 2)]
FIRST = [(2, 1), (1, 2), (0, 0), (3, 3)]


def inverse(pairs):
    return [(b, a) for a, b in pairs]


def gelu_pair(upper):
    inner = jnp.tanh(GELU_COEF * (upper + 0.044715 * upper * upper * upper))
    value = 0.5 * upper * (1.0 + inner)
    slope = 0.5 * (1.0 + inner) + 0.5 * upper * (1.0 - inner * inner) * GELU_COEF * (
        1.0 + 3.0 * 0.044715 * upper * upper
    )
    return value, slope


def norm_rowwise(values):
    mean = jnp.mean(values, axis=-1, keepdims=True)
    msq = jnp.mean(values * values, axis=-1, keepdims=True)
    rstd = lax.rsqrt(msq - mean * mean + NORM_EPS)
    return (values - mean) * rstd, rstd


def norm_backward(dnorm, normed, rstd):
    first = jnp.mean(dnorm, axis=-1, keepdims=True)
    second = jnp.mean(dnorm * normed, axis=-1, keepdims=True)
    return rstd * (dnorm - first - normed * second)


def halve_bit(block, bit, position):
    mine = (lax.axis_index("dp") // bit) % 2
    keep = lax.dynamic_index_in_dim(block, mine, position, keepdims=False)
    send = lax.dynamic_index_in_dim(block, 1 - mine, position, keepdims=False)
    return keep, bit_swap(send, bit)


def add(a, b):
    return narrowed(a.astype(F32) + b.astype(F32))


def dp_bits():
    size = lax.axis_size("dp")
    bits = []
    bit = 1
    while bit < size:
        bits.append(bit)
        bit *= 2
    return bits


def split_dp(block):
    bits = dp_bits()
    lead = block.shape[:-2]
    rows, cols = block.shape[-2:]
    return block.reshape(lead + (2,) * len(bits) + (rows // lax.axis_size("dp"), cols))


def scatter_bits(view, bits, last=True):
    for i, bit in enumerate(bits):
        keep, got = halve_bit(view, bit, view.ndim - 3)
        if last and i == len(bits) - 1:
            view = keep.astype(F32) + got.astype(F32)
        else:
            view = add(keep, got)
    return view


ROWS = 64
LANES = 256


def call(kernel, name, outs, meta, *args):
    vmem = pl.BlockSpec(memory_space=pltpu.VMEM)
    return pl.pallas_call(
        kernel,
        out_shape=[jax.ShapeDtypeStruct(shape, dtype) for shape, dtype in outs],
        in_specs=[pl.BlockSpec(memory_space=pltpu.SMEM)] + [vmem] * len(args),
        out_specs=[vmem] * len(outs),
        name=name,
    )(meta, *args)


def is_diag(meta):
    return meta[0] == meta[1]


def ordered(diag, mine, other):
    return jnp.concatenate([jnp.where(diag, mine, other), jnp.where(diag, other, mine)], axis=-1)


def block_of(diag, x, half):
    return jnp.where(diag, x[:, :half], x[:, half:])


def rows_of(ref_mine, ref_other, diag, i):
    part = slice(i * ROWS, (i + 1) * ROWS)
    return ordered(diag, ref_mine[part, :].astype(F32), ref_other[part, :].astype(F32))


def column_sum(x):
    return jnp.sum(x, axis=0, keepdims=True)


def mod_kernel(meta, cond, cond_o, w_ada, b_ada, b_proj, b_fc2, own, away, silu):
    diag = is_diag(meta)
    half = cond.shape[1]
    mine = jnp.where(diag, cond[...].astype(F32), cond_o[...].astype(F32))
    act = narrowed(mine / (1.0 + jnp.exp(-mine)))
    silu[...] = act.astype(F32)
    part = dot(act, w_ada[...])
    first = meta[0] == 0
    near = jnp.where(first, part[0:1], part[1:2])
    far = jnp.where(first, part[1:2], part[0:1])
    near = near + b_ada[...]
    for i in range(6):
        span = slice(i * half, (i + 1) * half)
        own[i : i + 1, :] = near[:, span]
        away[i : i + 1, :] = far[:, span]
    own[6:7, :] = b_proj[...]
    own[7:8, :] = b_fc2[...]
    away[6:8, :] = jnp.zeros((2, half), F32)


def attention_kernel(
    meta, tok_m, tok_o, own, got_col, got_row, got_cross, w_qkv, wq2, b_qv, wp_a, wp_b,
    mod_ref, h1_ref, qkv_ref, lse_ref, att_ref, bp_ref, bpb_ref,
):
    diag = is_diag(meta)
    half = tok_m.shape[1]
    seq = tok_m.shape[0]
    mod = ordered(diag, own[...] + got_row[...], got_col[...] + got_cross[...])
    mod_ref[...] = mod
    shift, scale = mod[0:1], mod[1:2]
    for i in range(seq // ROWS):
        n1, _ = norm_rowwise(rows_of(tok_m, tok_o, diag, i))
        h1_ref[i * ROWS : (i + 1) * ROWS, :] = narrowed(n1 * (1.0 + scale) + shift)
    for j in range(3):
        span = slice(j * half, (j + 1) * half)
        part = dot(h1_ref[:, :half], w_qkv[:, span]) + dot(h1_ref[:, half:], wq2[:, span])
        if j == 0:
            part = part + b_qv[0:1, :]
        if j == 2:
            part = part + b_qv[1:2, :]
        qkv_ref[:, span] = narrowed(part)
    for h in range(half // HEAD_SIZE):
        q, k, v = (qkv_ref[:, j * half + h * HEAD_SIZE : j * half + (h + 1) * HEAD_SIZE] for j in range(3))
        scores = dot_nt(q, k) * (HEAD_SIZE ** (-0.5))
        top = jnp.max(scores, axis=-1, keepdims=True)
        grown = jnp.exp(scores - top)
        total = jnp.sum(grown, axis=-1, keepdims=True)
        lse_ref[:, h : h + 1] = top + jnp.log(total)
        probs = narrowed(grown * (1.0 / total))
        att_ref[:, h * HEAD_SIZE : (h + 1) * HEAD_SIZE] = narrowed(dot(probs, v))
    for j, w in enumerate((wp_a, wp_b)):
        span = slice(j * half, (j + 1) * half)
        part = dot(att_ref[...], w[...])
        bp_ref[:, span] = part
        bpb_ref[:, span] = narrowed(part)


def mlp_kernel(
    meta, tok_m, tok_o, cot_m, cot_o, mod_ref, bp, bp_got, b_fc1, w_fc1, w12, w2_a, w2_b,
    br1_ref, h2_ref, dbr_ref, act_ref, dup_ref, keep_ref, send_ref, dh_ref, dhb_ref, gb1_ref,
):
    diag = is_diag(meta)
    half = tok_m.shape[1]
    seq = tok_m.shape[0]
    mod = mod_ref[...]
    gate1, shift, scale, gate2, bias = mod[2:3], mod[3:4], mod[4:5], mod[5:6], mod[6:7]
    for i in range(seq // ROWS):
        part = slice(i * ROWS, (i + 1) * ROWS)
        branch = bp[part, :] + bp_got[part, :].astype(F32) + bias
        br1_ref[part, :] = branch
        mid = rows_of(tok_m, tok_o, diag, i) + gate1 * branch
        n2, _ = norm_rowwise(mid)
        h2_ref[part, :] = narrowed(n2 * (1.0 + scale) + shift)
        dbr_ref[part, :] = narrowed(rows_of(cot_m, cot_o, diag, i) * gate2)
    for j in range(w_fc1.shape[1] // LANES):
        span = slice(j * LANES, (j + 1) * LANES)
        upper = dot(h2_ref[:, :half], w_fc1[:, span]) + dot(h2_ref[:, half:], w12[:, span]) + b_fc1[:, span]
        value, slope = gelu_pair(upper)
        act_ref[:, span] = narrowed(value)
        back = dot_nt(dbr_ref[:, :half], w2_a[span, :]) + dot_nt(dbr_ref[:, half:], w2_b[span, :])
        d_upper = back * slope
        gb1_ref[:, span] = column_sum(d_upper)
        dup_ref[:, span] = narrowed(d_upper)
    for j, w in enumerate((w_fc1, w12)):
        span = slice(j * half, (j + 1) * half)
        part = dot_nt(dup_ref[...], w[...])
        dh_ref[:, span] = part
        dhb_ref[:, span] = narrowed(part)
    down_a = dot(act_ref[...], w2_a[...])
    down_b = dot(act_ref[...], w2_b[...])
    keep_ref[...] = jnp.where(diag, down_a, down_b)
    send_ref[...] = narrowed(jnp.where(diag, down_b, down_a))


def output_kernel(meta, tok_m, cot_m, mod_ref, br1, keep, got, b_fc2, out_ref, sum_ref):
    diag = is_diag(meta)
    half = tok_m.shape[1]
    gate1, gate2 = (block_of(diag, mod_ref[i : i + 1, :], half) for i in (2, 5))
    first = jnp.zeros((1, half), F32)
    second = jnp.zeros((1, half), F32)
    for i in range(tok_m.shape[0] // ROWS):
        part = slice(i * ROWS, (i + 1) * ROWS)
        mid = tok_m[part, :].astype(F32) + gate1 * block_of(diag, br1[part, :], half)
        branch = keep[part, :] + got[part, :].astype(F32) + b_fc2[...]
        out_ref[part, :] = narrowed(mid + gate2 * branch)
        g = cot_m[part, :].astype(F32)
        first = first + column_sum(g * branch)
        second = second + column_sum(g * gate2)
    sum_ref[0:1, :] = first
    sum_ref[1:2, :] = second


def grad_kernel_rows(meta, left, right, first, second):
    half = left.shape[1] // 2
    first[...] = narrowed(dot_tn(left[:, :half], right[...]))
    second[...] = narrowed(dot_tn(left[:, half:], right[...]))


def grad_kernel_columns(meta, left, right, first, second):
    half = right.shape[1] // 2
    first[...] = narrowed(dot_tn(left[...], right[:, :half]))
    second[...] = narrowed(dot_tn(left[...], right[:, half:]))


def back_kernel(
    meta, tok_m, tok_o, cot_m, cot_o, mod_ref, br1, dh, dh_got, qkv, lse, wp_a, wp_b, w_qkv, wq2,
    dmid_ref, dbr_ref, dqkv_ref, dh1_ref, dh1b_ref, wide_ref, bias_ref, datt_ref,
):
    diag = is_diag(meta)
    half = tok_m.shape[1]
    seq = tok_m.shape[0]
    mod = mod_ref[...]
    gate1, scale2 = mod[2:3], mod[4:5]
    sums = [jnp.zeros((1, 2 * half), F32) for _ in range(4)]
    for i in range(seq // ROWS):
        part = slice(i * ROWS, (i + 1) * ROWS)
        branch = br1[part, :]
        n2, rstd2 = norm_rowwise(rows_of(tok_m, tok_o, diag, i) + gate1 * branch)
        d_h2 = dh[part, :] + dh_got[part, :].astype(F32)
        d_mid = rows_of(cot_m, cot_o, diag, i) + norm_backward(d_h2 * (1.0 + scale2), n2, rstd2)
        dmid_ref[part, :] = d_mid
        d_branch = d_mid * gate1
        dbr_ref[part, :] = narrowed(d_branch)
        for n, term in enumerate((d_mid * branch, d_h2, d_h2 * n2, d_branch)):
            sums[n] = sums[n] + column_sum(term)
    for n in range(4):
        wide_ref[n : n + 1, :] = sums[n]
    datt_ref[...] = narrowed(dot_nt(dbr_ref[:, :half], wp_a[...]) + dot_nt(dbr_ref[:, half:], wp_b[...]))
    root = HEAD_SIZE ** (-0.5)
    for h in range(half // HEAD_SIZE):
        q, k, v = (qkv[:, j * half + h * HEAD_SIZE : j * half + (h + 1) * HEAD_SIZE] for j in range(3))
        d_att = datt_ref[:, h * HEAD_SIZE : (h + 1) * HEAD_SIZE]
        probs = jnp.exp(dot_nt(q, k) * root - lse[:, h : h + 1])
        d_v = dot_tn(narrowed(probs), d_att)
        d_probs = dot_nt(d_att, v)
        d_scores = narrowed(probs * (d_probs - jnp.sum(probs * d_probs, axis=-1, keepdims=True)))
        d_q = dot(d_scores, k) * root
        d_k = dot_tn(d_scores, q) * root
        for j, term in enumerate((d_q, d_k, d_v)):
            dqkv_ref[:, j * half + h * HEAD_SIZE : j * half + (h + 1) * HEAD_SIZE] = narrowed(term)
        bias_ref[0:1, h * HEAD_SIZE : (h + 1) * HEAD_SIZE] = column_sum(d_q)
        bias_ref[1:2, h * HEAD_SIZE : (h + 1) * HEAD_SIZE] = column_sum(d_v)
    for j, w in enumerate((w_qkv, wq2)):
        span = slice(j * half, (j + 1) * half)
        part = dot_nt(dqkv_ref[...], w[...])
        dh1_ref[:, span] = part
        dh1b_ref[:, span] = narrowed(part)


def last_kernel(
    meta, tok_m, tok_o, mod_ref, d_mid, dh1, dh1_got, wide, bias, gb1, outs, grad_ref, mod_grad_ref, sum_ref,
):
    diag = is_diag(meta)
    half = tok_m.shape[1]
    scale1 = mod_ref[1:2, :]
    first = jnp.zeros((1, 2 * half), F32)
    second = jnp.zeros((1, 2 * half), F32)
    for i in range(tok_m.shape[0] // ROWS):
        part = slice(i * ROWS, (i + 1) * ROWS)
        n1, rstd1 = norm_rowwise(rows_of(tok_m, tok_o, diag, i))
        d_h1 = dh1[part, :] + dh1_got[part, :].astype(F32)
        grad = d_mid[part, :] + norm_backward(d_h1 * (1.0 + scale1), n1, rstd1)
        grad_ref[part, :] = narrowed(block_of(diag, grad, half))
        first = first + column_sum(d_h1)
        second = second + column_sum(d_h1 * n1)
    d_gate1, d_shift2, d_scale2, gb_proj = (wide[n : n + 1, :] for n in range(4))
    for n, term in enumerate((first, second, d_gate1, d_shift2, d_scale2)):
        mod_grad_ref[n : n + 1, :] = block_of(diag, term, half)
    mod_grad_ref[5:6, :] = outs[0:1, :]
    sum_ref[0:2, :] = bias[...]
    sum_ref[2:3, :] = block_of(diag, gb_proj, half)
    for n in range(gb1.shape[1] // half):
        sum_ref[3 + n : 4 + n, :] = gb1[:, n * half : (n + 1) * half]
    n = 3 + gb1.shape[1] // half
    sum_ref[n : n + 1, :] = outs[1:2, :]


def body(tokens, cond, w_ada, b_ada, w_qkv, b_qv, w_proj, b_proj, w_fc1, b_fc1, w_fc2, b_fc2, cotangent):
    r = lax.axis_index("row")
    c = lax.axis_index("col")
    diag = r == c
    meta = jnp.stack([r, c]).astype(jnp.int32)
    half = tokens.shape[1]
    seq = tokens.shape[0] // 2
    hidden = w_fc1.shape[1]
    three = 3 * half

    def own_tokens(x):
        return lax.dynamic_slice_in_dim(x, r * seq, seq, 0)

    def both_rows(x):
        other = row_swap(x)
        return jnp.concatenate(
            [jnp.where(r == 0, x, other), jnp.where(r == 0, other, x)], axis=0
        )

    cond_other = col_swap(cond)
    tok_m = own_tokens(tokens)
    tok_o = col_swap(tok_m)
    wq2 = row_swap(w_qkv)
    wp_b = lax.ppermute(w_proj, ("row", "col"), SECOND)
    wp_a = lax.ppermute(w_proj, ("row", "col"), FIRST)
    w12 = row_swap(w_fc1)
    w2_b = lax.ppermute(w_fc2, ("row", "col"), SECOND)
    w2_a = lax.ppermute(w_fc2, ("row", "col"), FIRST)
    cot_m = own_tokens(cotangent)
    cot_o = col_swap(cot_m)

    own, away, silu_r = call(
        mod_kernel, "modulate", [((8, half), F32), ((8, half), F32), ((2, half), F32)],
        meta, cond, cond_other, w_ada, b_ada[None], b_proj[None], b_fc2[None],
    )
    got_col = col_swap(own)
    got_row = row_swap(away)
    got_cross = cross_swap(away)
    mod, h1, qkv, lse, att, bp, bp_b = call(
        attention_kernel, "attention",
        [((8, 2 * half), F32), ((seq, 2 * half), BF16), ((seq, three), BF16), ((seq, 128), F32),
         ((seq, half), BF16), ((seq, 2 * half), F32), ((seq, 2 * half), BF16)],
        meta, tok_m, tok_o, own, got_col, got_row, got_cross, w_qkv, wq2, b_qv, wp_a, wp_b,
    )
    bp_got = col_swap(bp_b)
    br1, h2, d_br2, act, d_up, keep, send, dh2, dh2_b, gb1 = call(
        mlp_kernel, "mlp",
        [((seq, 2 * half), F32), ((seq, 2 * half), BF16), ((seq, 2 * half), BF16), ((seq, hidden), BF16),
         ((seq, hidden), BF16), ((seq, half), F32), ((seq, half), BF16), ((seq, 2 * half), F32),
         ((seq, 2 * half), BF16), ((1, hidden), F32)],
        meta, tok_m, tok_o, cot_m, cot_o, mod, bp, bp_got, b_fc1[None], w_fc1, w12, w2_a, w2_b,
    )
    dh2_got = col_swap(dh2_b)
    down_got = col_swap(send)
    g_fc2 = call(
        grad_kernel_columns, "grad_fc2", [((hidden, half), BF16)] * 2, meta, act, d_br2,
    )
    g_fc1 = call(
        grad_kernel_rows, "grad_fc1", [((half, hidden), BF16)] * 2, meta, h2, d_up,
    )
    d_mid, d_br1, d_qkv, dh1, dh1_b, wide, bias, _ = call(
        back_kernel, "back",
        [((seq, 2 * half), F32), ((seq, 2 * half), BF16), ((seq, three), BF16), ((seq, 2 * half), F32),
         ((seq, 2 * half), BF16), ((4, 2 * half), F32), ((2, half), F32), ((seq, half), BF16)],
        meta, tok_m, tok_o, cot_m, cot_o, mod, br1, dh2, dh2_got, qkv, lse, wp_a, wp_b, w_qkv, wq2,
    )
    dh1_got = col_swap(dh1_b)
    g_qkv = call(
        grad_kernel_rows, "grad_qkv", [((half, three), BF16)] * 2, meta, h1, d_qkv,
    )
    g_proj = call(
        grad_kernel_columns, "grad_proj", [((half, half), BF16)] * 2, meta, att, d_br1,
    )
    out_c, outs = call(
        output_kernel, "output", [((seq, half), BF16), ((2, half), F32)],
        meta, tok_m, cot_m, mod, br1, keep, down_got, b_fc2[None],
    )
    output = both_rows(out_c)
    tok_grad, d_mod, sums = call(
        last_kernel, "last", [((seq, half), BF16), ((6, half), F32), ((4 + hidden // half, half), F32)],
        meta, tok_m, tok_o, mod, d_mid, dh1, dh1_got, wide, bias, gb1, outs,
    )
    token_gradient = both_rows(tok_grad)

    bits = dp_bits()

    def column_form(first, second):
        return scatter_bits(split_dp(add(first, row_swap(second))), bits)

    def row_form(first, second):
        a = lax.ppermute(second, ("row", "col"), inverse(SECOND))
        b = lax.ppermute(first, ("row", "col"), inverse(FIRST))
        return scatter_bits(split_dp(add(a, b)), bits)

    out_fc2 = row_form(*g_fc2)[None]
    out_fc1 = column_form(*g_fc1)[None]
    out_proj = row_form(*g_proj)[None]
    out_qkv = column_form(*g_qkv)[None]

    latent = d_mod[None]
    got_latent, got_sums = row_swap((latent, sums))
    sums = sums + got_sums
    pair = jnp.concatenate([jnp.where(r == 0, latent, got_latent), jnp.where(r == 0, got_latent, latent)])
    d_mod_pair = narrowed(pair.reshape(2, 6 * half))
    pair = jnp.concatenate([pair, silu_r[:, None]], axis=1)
    d_cond = dot_nt(d_mod_pair, w_ada)
    d_cond = d_cond + col_swap(d_cond)
    d_cond = jnp.where(diag, d_cond, row_swap(d_cond))
    cond32 = cond.astype(F32)
    sig = jax.nn.sigmoid(cond32)
    grad_cond = narrowed(d_cond * sig * (1.0 + cond32 * (1.0 - sig)))
    for bit in bits:
        got_pair, got_sums = bit_swap((pair, sums), bit)
        pair = jnp.concatenate([pair, got_pair])
        sums = sums + got_sums
    n_all = pair.shape[0]
    d_mod_all = pair[:, :6].reshape(n_all, 6 * half)
    rows = half // lax.axis_size("dp")
    silu_rows = narrowed(lax.dynamic_slice_in_dim(pair[:, 6], lax.axis_index("dp") * rows, rows, 1))
    out_ada = dot_tn(silu_rows, narrowed(d_mod_all))[None]
    out_b_ada = jnp.sum(d_mod_all, axis=0)
    out_b_qv = sums[:2]
    out_b_proj = sums[2]
    out_b_fc1 = sums[3:-1].reshape(-1)
    out_b_fc2 = sums[-1]
    return (
        output, token_gradient, grad_cond, out_ada, out_b_ada, out_qkv, out_b_qv,
        out_proj, out_b_proj, out_fc1, out_b_fc1, out_fc2, out_b_fc2,
    )


def solution(mesh):
    in_specs = (
        P("dp", "col"), P("dp", "col"), P("row", "col"), P("col"), P("row", "col"), P(None, "col"),
        P("row", "col"), P("col"), P("row", "col"), P("col"), P("row", "col"), P("col"), P("dp", "col"),
    )
    out_specs = (
        P("dp", "col"), P("dp", "col"), P("dp", "col"), P("row", "dp", "col"), P("col"),
        P("row", "dp", "col"), P(None, "col"), P("row", "dp", "col"), P("col"), P("row", "dp", "col"),
        P("col"), P("row", "dp", "col"), P("col"),
    )
    return jax.shard_map(body, mesh=mesh, in_specs=in_specs, out_specs=out_specs, check_vma=False)
```

```python
import functools

import jax
import jax.numpy as jnp
from jax import lax
from jax.experimental import pallas as pl
from jax.experimental.pallas import tpu as pltpu
from jax.sharding import PartitionSpec as P


HEAD_SIZE = 64
NORM_EPS = 1e-06
GELU_COEF = 0.7978845608028654
F32 = jnp.float32
BF16 = jnp.bfloat16


def narrowed(values):
    return values.astype(BF16)


def dot(a, b):
    return jnp.dot(a, b, preferred_element_type=F32)


def dot_nt(a, b):
    return lax.dot_general(a, b, (((1,), (1,)), ((), ())), preferred_element_type=F32)


def dot_tn(a, b):
    return lax.dot_general(a, b, (((0,), (0,)), ((), ())), preferred_element_type=F32)


def col_swap(x):
    return lax.ppermute(x, "col", [(0, 1), (1, 0)])


def row_swap(x):
    return lax.ppermute(x, "row", [(0, 1), (1, 0)])


def cross_swap(x):
    return lax.ppermute(x, ("row", "col"), [(0, 3), (1, 2), (2, 1), (3, 0)])


def bit_swap(x, bit):
    size = lax.axis_size("dp")
    return lax.ppermute(x, "dp", [(i, i ^ bit) for i in range(size)])


def off_diagonal_swap(x, bit):
    size = lax.axis_size("dp")
    pairs = [(4 * i + n, 4 * (i ^ bit) + n) for i in range(size) for n in (1, 2)]
    return lax.ppermute(x, ("dp", "row", "col"), pairs)


SECOND = [(1, 0), (2, 3), (3, 1), (0, 2)]
FIRST = [(2, 1), (1, 2)]


def inverse(pairs):
    return [(b, a) for a, b in pairs]


def gelu_pair(upper):
    inner = jnp.tanh(GELU_COEF * (upper + 0.044715 * upper * upper * upper))
    value = 0.5 * upper * (1.0 + inner)
    slope = 0.5 * (1.0 + inner) + 0.5 * upper * (1.0 - inner * inner) * GELU_COEF * (
        1.0 + 3.0 * 0.044715 * upper * upper
    )
    return value, slope


def norm_rowwise(values):
    mean = jnp.mean(values, axis=-1, keepdims=True)
    msq = jnp.mean(values * values, axis=-1, keepdims=True)
    rstd = lax.rsqrt(msq - mean * mean + NORM_EPS)
    return (values - mean) * rstd, rstd


def norm_backward(dnorm, normed, rstd):
    first = jnp.mean(dnorm, axis=-1, keepdims=True)
    second = jnp.mean(dnorm * normed, axis=-1, keepdims=True)
    return rstd * (dnorm - first - normed * second)


def halve_bit(block, bit, position):
    mine = (lax.axis_index("dp") // bit) % 2
    keep = lax.dynamic_index_in_dim(block, mine, position, keepdims=False)
    send = lax.dynamic_index_in_dim(block, 1 - mine, position, keepdims=False)
    got = bit_swap(send, bit)
    return keep, got


def add(a, b):
    return narrowed(a.astype(F32) + b.astype(F32))


def dp_bits():
    size = lax.axis_size("dp")
    bits = []
    bit = 1
    while bit < size:
        bits.append(bit)
        bit *= 2
    return bits


def split_dp(block):
    bits = dp_bits()
    lead = block.shape[:-2]
    rows, cols = block.shape[-2:]
    return block.reshape(lead + (2,) * len(bits) + (rows // lax.axis_size("dp"), cols))


def scatter_bits(view, bits):
    for i, bit in enumerate(bits):
        keep, got = halve_bit(view, bit, view.ndim - 3)
        if i == len(bits) - 1:
            view = keep.astype(F32) + got.astype(F32)
        else:
            view = add(keep, got)
    return view


ROWS = 64
LANES = 256


def call(kernel, outs, meta, *args, scratch=()):
    vmem = pl.BlockSpec(memory_space=pltpu.VMEM)
    return pl.pallas_call(
        kernel,
        out_shape=[jax.ShapeDtypeStruct(shape, dtype) for shape, dtype in outs],
        in_specs=[pl.BlockSpec(memory_space=pltpu.SMEM)] + [vmem] * len(args),
        out_specs=[vmem] * len(outs),
        scratch_shapes=[pltpu.VMEM(shape, dtype) for shape, dtype in scratch],
    )(meta, *args)


def is_diag(meta):
    return meta[0] == meta[1]


def ordered(diag, mine, other):
    return jnp.concatenate([jnp.where(diag, mine, other), jnp.where(diag, other, mine)], axis=-1)


def block_of(diag, x, half):
    return jnp.where(diag, x[:, :half], x[:, half:])


def rows_of(ref_mine, ref_other, diag, i, base=0):
    part = slice(base + i * ROWS, base + (i + 1) * ROWS)
    return ordered(diag, ref_mine[part, :].astype(F32), ref_other[part, :].astype(F32))


def join(scratch, bit, mine, other):
    n = mine.shape[0]
    scratch[pl.ds(pl.multiple_of(bit * n, n), n), :] = mine[...]
    scratch[pl.ds(pl.multiple_of((1 - bit) * n, n), n), :] = other[...]


def column_sum(x):
    return jnp.sum(x, axis=0, keepdims=True)


def mod_kernel(meta, cond, cond_o, w_ada, bias8, own, away, silu):
    diag = is_diag(meta)
    half = cond.shape[1]
    mine = jnp.where(diag, cond[...].astype(F32), cond_o[...].astype(F32))
    act = narrowed(mine / (1.0 + jnp.exp(-mine)))
    silu[...] = act.astype(F32)
    part = dot(act, w_ada[...])
    first = meta[0] == 0
    near = jnp.where(first, part[0:1], part[1:2])
    far = jnp.where(first, part[1:2], part[0:1])
    for i in range(6):
        span = slice(i * half, (i + 1) * half)
        own[i : i + 1, :] = near[:, span] + bias8[i : i + 1, :]
        away[i : i + 1, :] = far[:, span]
    own[6:8, :] = bias8[6:8, :]
    away[6:8, :] = jnp.zeros((2, half), F32)


def attention_kernel(
    meta, tc_m, tc_o, own, got_col, got_row, got_cross, w_qkv, wq_m, wq_o, b_qv, w_proj, wp_f, wp_b,
    mod_ref, h1_ref, qkv_ref, lse_ref, att_ref, bp_ref, bpb_ref, wq2, wp_a,
):
    diag = is_diag(meta)
    join(wq2, meta[2], wq_m, wq_o)
    wp_a[...] = jnp.where(diag, w_proj[...], wp_f[...])
    half = tc_m.shape[1]
    seq = tc_m.shape[0] // 2
    mod = ordered(diag, own[...] + got_row[...], got_col[...] + got_cross[...])
    mod_ref[...] = mod
    shift, scale = mod[0:1], mod[1:2]
    for i in range(seq // ROWS):
        n1, _ = norm_rowwise(rows_of(tc_m, tc_o, diag, i))
        h1_ref[i * ROWS : (i + 1) * ROWS, :] = narrowed(n1 * (1.0 + scale) + shift)
    for j in range(3):
        span = slice(j * half, (j + 1) * half)
        part = dot(h1_ref[:, :half], w_qkv[:, span]) + dot(h1_ref[:, half:], wq2[:, span])
        if j == 0:
            part = part + b_qv[0:1, :]
        if j == 2:
            part = part + b_qv[1:2, :]
        qkv_ref[:, span] = narrowed(part)
    for h in range(half // HEAD_SIZE):
        q, k, v = (qkv_ref[:, j * half + h * HEAD_SIZE : j * half + (h + 1) * HEAD_SIZE] for j in range(3))
        scores = dot_nt(q, k) * (HEAD_SIZE ** (-0.5))
        top = jnp.max(scores, axis=-1, keepdims=True)
        grown = jnp.exp(scores - top)
        total = jnp.sum(grown, axis=-1, keepdims=True)
        lse_ref[:, h : h + 1] = top + jnp.log(total)
        probs = narrowed(grown * (1.0 / total))
        att_ref[:, h * HEAD_SIZE : (h + 1) * HEAD_SIZE] = narrowed(dot(probs, v))
    for j, w in enumerate((wp_a, wp_b)):
        span = slice(j * half, (j + 1) * half)
        part = dot(att_ref[...], w[...])
        bp_ref[:, span] = part
        bpb_ref[:, span] = narrowed(part)


def mlp_kernel(
    meta, tc_m, tc_o, mod_ref, bp, bp_got, b_fc1, w_fc1, w1_m, w1_o, w_fc2, w2_d, w2f_m, w2f_o, w2s_m, w2s_o,
    br1_ref, h2_ref, dbr_ref, act_ref, dup_ref, keep_ref, send_ref, dh_ref, dhb_ref, gb1_ref, w12, w2_a, w2_b,
):
    diag = is_diag(meta)
    join(w12, meta[2], w1_m, w1_o)

    @pl.when(diag)
    def _():
        w2_a[...] = w_fc2[...]
        w2_b[...] = w2_d[...]

    @pl.when(jnp.logical_not(diag))
    def _():
        join(w2_a, meta[3], w2f_m, w2f_o)
        join(w2_b, meta[3], w2s_m, w2s_o)

    half = tc_m.shape[1]
    seq = tc_m.shape[0] // 2
    mod = mod_ref[...]
    gate1, shift, scale, gate2, bias = mod[2:3], mod[3:4], mod[4:5], mod[5:6], mod[6:7]
    for i in range(seq // ROWS):
        part = slice(i * ROWS, (i + 1) * ROWS)
        branch = bp[part, :] + bp_got[part, :].astype(F32) + bias
        br1_ref[part, :] = branch
        mid = rows_of(tc_m, tc_o, diag, i) + gate1 * branch
        n2, _ = norm_rowwise(mid)
        h2_ref[part, :] = narrowed(n2 * (1.0 + scale) + shift)
        dbr_ref[part, :] = narrowed(rows_of(tc_m, tc_o, diag, i, seq) * gate2)
    for j in range(w_fc1.shape[1] // LANES):
        span = slice(j * LANES, (j + 1) * LANES)
        upper = dot(h2_ref[:, :half], w_fc1[:, span]) + dot(h2_ref[:, half:], w12[:, span]) + b_fc1[:, span]
        value, slope = gelu_pair(upper)
        act_ref[:, span] = narrowed(value)
        back = dot_nt(dbr_ref[:, :half], w2_a[span, :]) + dot_nt(dbr_ref[:, half:], w2_b[span, :])
        d_upper = back * slope
        gb1_ref[:, span] = column_sum(d_upper)
        dup_ref[:, span] = narrowed(d_upper)
    for j, w in enumerate((w_fc1, w12)):
        span = slice(j * half, (j + 1) * half)
        part = dot_nt(dup_ref[...], w[...])
        dh_ref[:, span] = part
        dhb_ref[:, span] = narrowed(part)
    down_a = dot(act_ref[...], w2_a[...])
    down_b = dot(act_ref[...], w2_b[...])
    keep_ref[...] = jnp.where(diag, down_a, down_b)
    send_ref[...] = narrowed(jnp.where(diag, down_b, down_a))


def output_kernel(meta, tc_m, mod_ref, br1, keep, got, b_fc2, out_ref, sum_ref):
    diag = is_diag(meta)
    half = tc_m.shape[1]
    gate1, gate2 = (block_of(diag, mod_ref[i : i + 1, :], half) for i in (2, 5))
    first = jnp.zeros((1, half), F32)
    second = jnp.zeros((1, half), F32)
    seq = tc_m.shape[0] // 2
    for i in range(seq // ROWS):
        part = slice(i * ROWS, (i + 1) * ROWS)
        mid = tc_m[part, :].astype(F32) + gate1 * block_of(diag, br1[part, :], half)
        branch = keep[part, :] + got[part, :].astype(F32) + b_fc2[...]
        out_ref[part, :] = narrowed(mid + gate2 * branch)
        g = tc_m[seq + i * ROWS : seq + (i + 1) * ROWS, :].astype(F32)
        first = first + column_sum(g * branch)
        second = second + column_sum(g * gate2)
    sum_ref[0:1, :] = first
    sum_ref[1:2, :] = second


def write_halves(bit, block, source, n, keep, send):
    for k in range(source.shape[0] // (2 * block)):
        part = slice(k * block, (k + 1) * block)
        keep[n, part, :] = source[pl.ds(pl.multiple_of((2 * k + bit) * block, block), block), :]
        send[n, part, :] = source[pl.ds(pl.multiple_of((2 * k + 1 - bit) * block, block), block), :]


def fc2_grad_kernel(block, meta, act, d_branch, *refs):
    half = d_branch.shape[1] // 2
    for n in range(2):
        part = narrowed(dot_tn(act[...], d_branch[:, n * half : (n + 1) * half]))
        if block:
            refs[2][...] = part
            write_halves(meta[2], block, refs[2], n, refs[0], refs[1])
        else:
            refs[0][n] = part


def fc1_grad_kernel(meta, hidden, d_upper, first, second):
    half = hidden.shape[1] // 2
    first[...] = narrowed(dot_tn(hidden[:, :half], d_upper[...]))
    second[...] = narrowed(dot_tn(hidden[:, half:], d_upper[...]))


def attention_grad_kernel(block, meta, hidden, d_qkv, att, d_branch, v_first, v_second, p_first, p_second, *refs):
    half = hidden.shape[1] // 2
    for n, (v, p) in enumerate(((v_first, p_first), (v_second, p_second))):
        span = slice(n * half, (n + 1) * half)
        v[...] = narrowed(dot_tn(hidden[:, span], d_qkv[:, 2 * half :]))
        p[...] = narrowed(dot_tn(att[...], d_branch[:, span]))
        part = narrowed(dot_tn(hidden[:, span], d_qkv[:, : 2 * half]))
        if block:
            refs[2][...] = part
            write_halves(meta[2], block, refs[2], n, refs[0], refs[1])
        else:
            refs[0][n] = part


def back_kernel(
    meta, tc_m, tc_o, mod_ref, br1, dh, dh_got, qkv, lse, w_proj, wp_f, wp_b, w_qkv, wq_m, wq_o,
    dmid_ref, dbr_ref, dqkv_ref, dh1_ref, dh1b_ref, wide_ref, bias_ref, datt_ref, wq2, wp_a,
):
    diag = is_diag(meta)
    join(wq2, meta[2], wq_m, wq_o)
    wp_a[...] = jnp.where(diag, w_proj[...], wp_f[...])
    half = tc_m.shape[1]
    seq = tc_m.shape[0] // 2
    mod = mod_ref[...]
    gate1, scale2 = mod[2:3], mod[4:5]
    sums = [jnp.zeros((1, 2 * half), F32) for _ in range(4)]
    for i in range(seq // ROWS):
        part = slice(i * ROWS, (i + 1) * ROWS)
        branch = br1[part, :]
        n2, rstd2 = norm_rowwise(rows_of(tc_m, tc_o, diag, i) + gate1 * branch)
        d_h2 = dh[part, :] + dh_got[part, :].astype(F32)
        d_mid = rows_of(tc_m, tc_o, diag, i, seq) + norm_backward(d_h2 * (1.0 + scale2), n2, rstd2)
        dmid_ref[part, :] = d_mid
        d_branch = d_mid * gate1
        dbr_ref[part, :] = narrowed(d_branch)
        for n, term in enumerate((d_mid * branch, d_h2, d_h2 * n2, d_branch)):
            sums[n] = sums[n] + column_sum(term)
    for n in range(4):
        wide_ref[n : n + 1, :] = sums[n]
    datt_ref[...] = narrowed(dot_nt(dbr_ref[:, :half], wp_a[...]) + dot_nt(dbr_ref[:, half:], wp_b[...]))
    root = HEAD_SIZE ** (-0.5)
    for h in range(half // HEAD_SIZE):
        q, k, v = (qkv[:, j * half + h * HEAD_SIZE : j * half + (h + 1) * HEAD_SIZE] for j in range(3))
        d_att = datt_ref[:, h * HEAD_SIZE : (h + 1) * HEAD_SIZE]
        probs = jnp.exp(dot_nt(q, k) * root - lse[:, h : h + 1])
        d_v = dot_tn(narrowed(probs), d_att)
        d_probs = dot_nt(d_att, v)
        d_scores = narrowed(probs * (d_probs - jnp.sum(probs * d_probs, axis=-1, keepdims=True)))
        d_q = dot(d_scores, k) * root
        d_k = dot_tn(d_scores, q) * root
        for j, term in enumerate((d_q, d_k, d_v)):
            dqkv_ref[:, j * half + h * HEAD_SIZE : j * half + (h + 1) * HEAD_SIZE] = narrowed(term)
        bias_ref[0:1, h * HEAD_SIZE : (h + 1) * HEAD_SIZE] = column_sum(d_q)
        bias_ref[1:2, h * HEAD_SIZE : (h + 1) * HEAD_SIZE] = column_sum(d_v)
    for j, w in enumerate((w_qkv, wq2)):
        span = slice(j * half, (j + 1) * half)
        part = dot_nt(dqkv_ref[...], w[...])
        dh1_ref[:, span] = part
        dh1b_ref[:, span] = narrowed(part)


def last_kernel(meta, tc_m, tc_o, mod_ref, d_mid, dh1, dh1_got, wide, bias, gb1, outs, silu, grad_ref, pay_ref):
    diag = is_diag(meta)
    half = tc_m.shape[1]
    scale1 = mod_ref[1:2, :]
    first = jnp.zeros((1, 2 * half), F32)
    second = jnp.zeros((1, 2 * half), F32)
    for i in range(tc_m.shape[0] // 2 // ROWS):
        part = slice(i * ROWS, (i + 1) * ROWS)
        n1, rstd1 = norm_rowwise(rows_of(tc_m, tc_o, diag, i))
        d_h1 = dh1[part, :] + dh1_got[part, :].astype(F32)
        grad = d_mid[part, :] + norm_backward(d_h1 * (1.0 + scale1), n1, rstd1)
        grad_ref[part, :] = narrowed(block_of(diag, grad, half))
        first = first + column_sum(d_h1)
        second = second + column_sum(d_h1 * n1)
    d_gate1, d_shift2, d_scale2, gb_proj = (block_of(diag, wide[n : n + 1, :], half) for n in range(4))
    first, second = (block_of(diag, term, half) for term in (first, second))
    roles = (first, second, d_gate1, d_shift2, d_scale2, outs[0:1, :], silu[0:1, :], silu[1:2, :])
    for n, term in enumerate(roles):
        pay_ref[0:1, n * half : (n + 1) * half] = term
    for n, term in enumerate((bias[0:1, :], bias[1:2, :], gb_proj, outs[1:2, :])):
        pay_ref[1:2, n * half : (n + 1) * half] = term
    pay_ref[1:2, 4 * half :] = gb1[...]


def finish_kernel(meta, own, got, w_ada, cond_ref, sum_ref, b_ada_ref, ada_ref):
    half = w_ada.shape[0]
    n = own.shape[0] - 1
    six = 6 * half
    first = meta[0] == 0
    sum_ref[...] = own[n : n + 1, :] + got[n : n + 1, :]
    near, far = own[:n, :six], got[:n, :six]
    b_ada_ref[...] = column_sum(near) + column_sum(far)
    pair = jnp.concatenate([jnp.where(first, near[:1], far[:1]), jnp.where(first, far[:1], near[:1])])
    cond_ref[...] = dot_nt(narrowed(pair), w_ada[...])
    rows = ada_ref.shape[0]
    spot = lax.broadcasted_iota(jnp.int32, (rows, half), 1) - lax.broadcasted_iota(jnp.int32, (rows, half), 0)
    select = narrowed(jnp.where(spot == meta[4] * rows, 1.0, 0.0))
    silu_0, silu_1 = narrowed(own[:n, six : six + half]), narrowed(own[:n, six + half : six + 2 * half])
    total = jnp.zeros(ada_ref.shape, F32)
    for values, silu in ((near, jnp.where(first, silu_0, silu_1)), (far, jnp.where(first, silu_1, silu_0))):
        total = total + dot(narrowed(dot_nt(select, silu)), narrowed(values))
    ada_ref[...] = total


def body(tokens, cond, w_ada, b_ada, w_qkv, b_qv, w_proj, b_proj, w_fc1, b_fc1, w_fc2, b_fc2, cotangent):
    r = lax.axis_index("row")
    c = lax.axis_index("col")
    diag = r == c
    d = lax.axis_index("dp")
    bits = dp_bits()
    bit_x, bit_z = bits[0], bits[min(1, len(bits) - 1)]
    bx, bz = (d // bit_x) % 2, (d // bit_z) % 2
    meta = jnp.stack([r, c, bx, bz, d]).astype(jnp.int32)
    half = tokens.shape[1]
    seq = tokens.shape[0] // 2
    hidden = w_fc1.shape[1]
    three = 3 * half

    def own_tokens(x):
        return lax.dynamic_slice_in_dim(x, r * seq, seq, 0)

    def both_rows(x):
        other = row_swap(x)
        return assembled(x, other)

    def assembled(x, other):
        return jnp.concatenate(
            [jnp.where(r == 0, x, other), jnp.where(r == 0, other, x)], axis=0
        )

    def half_rows(w, bit):
        n = w.shape[0] // 2
        return lax.dynamic_slice_in_dim(w, bit * n, n, 0)

    cond_other = col_swap(cond)
    tc_m = jnp.concatenate([own_tokens(tokens), own_tokens(cotangent)])
    tc_o = col_swap(tc_m)
    wp_b = lax.ppermute(w_proj, ("row", "col"), SECOND)
    wp_f = lax.ppermute(w_proj, ("row", "col"), FIRST)
    bias8 = jnp.concatenate([b_ada.reshape(6, half), b_proj[None], b_fc2[None]])

    own, away, silu_r = call(
        mod_kernel, [((8, half), F32), ((8, half), F32), ((2, half), F32)],
        meta, cond, cond_other, w_ada, bias8,
    )
    got_col = col_swap(own)
    got_row = row_swap(away)
    got_cross = cross_swap(away)
    wq_m = row_swap(half_rows(w_qkv, bx))
    w1_m = row_swap(half_rows(w_fc1, bx))
    w2_half = half_rows(w_fc2, bz)
    w2s_m = lax.ppermute(w2_half, ("row", "col"), [(3, 1), (0, 2)])
    w2f_m = lax.ppermute(w2_half, ("row", "col"), FIRST)
    w2_d = lax.ppermute(w_fc2, ("row", "col"), [(1, 0), (2, 3)])
    wq_o = bit_swap(wq_m, bit_x)
    w1_o = bit_swap(w1_m, bit_x)
    w2s_o = off_diagonal_swap(w2s_m, bit_z)
    w2f_o = off_diagonal_swap(w2f_m, bit_z)
    mod, h1, qkv, lse, att, bp, bp_b = call(
        attention_kernel,
        [((8, 2 * half), F32), ((seq, 2 * half), BF16), ((seq, three), BF16), ((seq, 128), F32),
         ((seq, half), BF16), ((seq, 2 * half), F32), ((seq, 2 * half), BF16)],
        meta, tc_m, tc_o, own, got_col, got_row, got_cross, w_qkv, wq_m, wq_o, b_qv,
        w_proj, wp_f, wp_b, scratch=[(w_qkv.shape, BF16), (w_proj.shape, BF16)],
    )
    bp_got = col_swap(bp_b)
    br1, h2, d_br2, act, d_up, keep, send, dh2, dh2_b, gb1 = call(
        mlp_kernel,
        [((seq, 2 * half), F32), ((seq, 2 * half), BF16), ((seq, 2 * half), BF16), ((seq, hidden), BF16),
         ((seq, hidden), BF16), ((seq, half), F32), ((seq, half), BF16), ((seq, 2 * half), F32),
         ((seq, 2 * half), BF16), ((1, hidden), F32)],
        meta, tc_m, tc_o, mod, bp, bp_got, b_fc1[None], w_fc1, w1_m, w1_o, w_fc2,
        w2_d, w2f_m, w2f_o, w2s_m, w2s_o,
        scratch=[(w_fc1.shape, BF16), (w_fc2.shape, BF16), (w_fc2.shape, BF16)],
    )
    dh2_got = col_swap(dh2_b)
    down_got = col_swap(send)

    def whole_or_halves(rows, cols):
        block = rows // lax.axis_size("dp") * bit_x
        if block % 16:
            return 0, [((2, rows, cols), BF16)], ()
        return block, [((2, rows // 2, cols), BF16)] * 2, [((rows, cols), BF16)]

    block, outs_fc2, scratch = whole_or_halves(hidden, half)
    g_fc2 = call(functools.partial(fc2_grad_kernel, block), outs_fc2, meta, act, d_br2, scratch=scratch)
    g_fc1 = call(fc1_grad_kernel, [((half, hidden), BF16)] * 2, meta, h2, d_up)
    d_mid, d_br1, d_qkv, dh1, dh1_b, wide, bias, _ = call(
        back_kernel,
        [((seq, 2 * half), F32), ((seq, 2 * half), BF16), ((seq, three), BF16), ((seq, 2 * half), F32),
         ((seq, 2 * half), BF16), ((4, 2 * half), F32), ((2, half), F32), ((seq, half), BF16)],
        meta, tc_m, tc_o, mod, br1, dh2, dh2_got, qkv, lse, w_proj, wp_f, wp_b,
        w_qkv, wq_m, wq_o, scratch=[(w_qkv.shape, BF16), (w_proj.shape, BF16)],
    )
    dh1_got = col_swap(dh1_b)
    block, outs_qk, scratch = whole_or_halves(half, 2 * half)
    v_1, v_2, p_1, p_2, *g_qk = call(
        functools.partial(attention_grad_kernel, block), [((half, half), BF16)] * 4 + outs_qk,
        meta, h1, d_qkv, att, d_br1, scratch=scratch,
    )
    out_c, outs = call(
        output_kernel, [((seq, half), BF16), ((2, half), F32)],
        meta, tc_m, mod, br1, keep, down_got, b_fc2[None],
    )
    output = both_rows(out_c)
    tok_grad, pay = call(
        last_kernel, [((seq, half), BF16), ((2, 4 * half + hidden), F32)],
        meta, tc_m, tc_o, mod, d_mid, dh1, dh1_got, wide, bias, gb1, outs, silu_r,
    )
    token_gradient = both_rows(tok_grad)

    def by_column(first, second):
        got = row_swap(second)
        return add(first, got)

    def by_row(first, second):
        near = lax.ppermute(second, ("row", "col"), inverse(SECOND))
        far = lax.ppermute(first, ("row", "col"), inverse(FIRST))
        return add(near, jnp.where(diag, first, far))

    def over_x(pair, rows):
        if len(pair) == 1:
            view = split_dp(pair[0])
            view = add(*halve_bit(view, bits[0], view.ndim - 3))
        else:
            got = bit_swap(pair[1], bits[0])
            shape = (2,) * (len(bits) - 1) + (rows // lax.axis_size("dp"), got.shape[-1])
            view = [add(pair[0][n], got[n]).reshape(shape) for n in range(2)]
        return view[0], view[1]

    fc1 = split_dp(by_column(*g_fc1))
    for bit in bits[1:]:
        fc1 = add(*halve_bit(fc1, bit, fc1.ndim - 4))
    out_fc1 = scatter_bits(fc1, bits[:1])[None]
    fc2 = by_row(*over_x(g_fc2, hidden))
    out_fc2 = scatter_bits(fc2, bits[1:])[None]
    qk = by_column(*over_x(g_qk, half))
    out_qk = scatter_bits(qk, bits[1:])
    vp = jnp.concatenate([by_column(v_1, v_2), by_row(p_1, p_2)], axis=-1)
    vp = scatter_bits(split_dp(vp), bits)
    out_proj = vp[:, half:][None]
    out_qkv = jnp.concatenate([out_qk, vp[:, :half]], axis=-1)[None]

    for bit in bits[1:] + bits[:1]:
        got = bit_swap(pay, bit)
        pay = jnp.concatenate([pay[:-1], got[:-1], pay[-1:] + got[-1:]])
    got = row_swap(pay)
    d_cond, sums, out_b_ada, out_ada = call(
        finish_kernel,
        [((2, half), F32), ((1, 4 * half + hidden), F32), ((1, 6 * half), F32), ((half // lax.axis_size("dp"), 6 * half), F32)],
        meta, pay, got, w_ada,
    )
    out_b_ada, out_ada = out_b_ada[0], out_ada[None]
    d_cond = d_cond + col_swap(d_cond)
    d_cond = jnp.where(diag, d_cond, row_swap(d_cond))
    cond32 = cond.astype(F32)
    sig = jax.nn.sigmoid(cond32)
    grad_cond = narrowed(d_cond * sig * (1.0 + cond32 * (1.0 - sig)))
    out_b_qv = sums[:, : 2 * half].reshape(2, half)
    out_b_proj = sums[0, 2 * half : 3 * half]
    out_b_fc2 = sums[0, 3 * half : 4 * half]
    out_b_fc1 = sums[0, 4 * half :]
    return (
        output, token_gradient, grad_cond, out_ada, out_b_ada, out_qkv, out_b_qv,
        out_proj, out_b_proj, out_fc1, out_b_fc1, out_fc2, out_b_fc2,
    )


def solution(mesh):
    in_specs = (
        P("dp", "col"), P("dp", "col"), P("row", "col"), P("col"), P("row", "col"), P(None, "col"),
        P("row", "col"), P("col"), P("row", "col"), P("col"), P("row", "col"), P("col"), P("dp", "col"),
    )
    out_specs = (
        P("dp", "col"), P("dp", "col"), P("dp", "col"), P("row", "dp", "col"), P("col"),
        P("row", "dp", "col"), P(None, "col"), P("row", "dp", "col"), P("col"), P("row", "dp", "col"),
        P("col"), P("row", "dp", "col"), P("col"),
    )
    return jax.shard_map(body, mesh=mesh, in_specs=in_specs, out_specs=out_specs, check_vma=False)
```

```python
import functools

import jax
import jax.numpy as jnp
from jax import lax
from jax.experimental import pallas as pl
from jax.experimental.pallas import tpu as pltpu
from jax.sharding import PartitionSpec as P


HEAD_SIZE = 64
NORM_EPS = 1e-06
GELU_COEF = 0.7978845608028654
F32 = jnp.float32
BF16 = jnp.bfloat16


def narrowed(values):
    return values.astype(BF16)


def dot(a, b):
    return jnp.dot(a, b, preferred_element_type=F32)


def dot_nt(a, b):
    return lax.dot_general(a, b, (((1,), (1,)), ((), ())), preferred_element_type=F32)


def dot_tn(a, b):
    return lax.dot_general(a, b, (((0,), (0,)), ((), ())), preferred_element_type=F32)


def col_swap(x):
    return lax.ppermute(x, "col", [(0, 1), (1, 0)])


def row_swap(x):
    return lax.ppermute(x, "row", [(0, 1), (1, 0)])


def cross_swap(x):
    return lax.ppermute(x, ("row", "col"), [(0, 3), (1, 2), (2, 1), (3, 0)])


def bit_swap(x, bit):
    size = lax.axis_size("dp")
    return lax.ppermute(x, "dp", [(i, i ^ bit) for i in range(size)])


def off_diagonal_swap(x, bit):
    size = lax.axis_size("dp")
    pairs = [(4 * i + n, 4 * (i ^ bit) + n) for i in range(size) for n in (1, 2)]
    return lax.ppermute(x, ("dp", "row", "col"), pairs)


SECOND = [(1, 0), (2, 3), (3, 1), (0, 2)]
FIRST = [(2, 1), (1, 2)]


def inverse(pairs):
    return [(b, a) for a, b in pairs]


def gelu_pair(upper):
    inner = jnp.tanh(GELU_COEF * (upper + 0.044715 * upper * upper * upper))
    value = 0.5 * upper * (1.0 + inner)
    slope = 0.5 * (1.0 + inner) + 0.5 * upper * (1.0 - inner * inner) * GELU_COEF * (
        1.0 + 3.0 * 0.044715 * upper * upper
    )
    return value, slope


def norm_rowwise(values):
    mean = jnp.mean(values, axis=-1, keepdims=True)
    msq = jnp.mean(values * values, axis=-1, keepdims=True)
    rstd = lax.rsqrt(msq - mean * mean + NORM_EPS)
    return (values - mean) * rstd, rstd


def norm_backward(dnorm, normed, rstd):
    first = jnp.mean(dnorm, axis=-1, keepdims=True)
    second = jnp.mean(dnorm * normed, axis=-1, keepdims=True)
    return rstd * (dnorm - first - normed * second)


def halve_bit(block, bit, position):
    mine = (lax.axis_index("dp") // bit) % 2
    keep = lax.dynamic_index_in_dim(block, mine, position, keepdims=False)
    send = lax.dynamic_index_in_dim(block, 1 - mine, position, keepdims=False)
    got = bit_swap(send, bit)
    return keep, got


def add(a, b):
    return narrowed(a.astype(F32) + b.astype(F32))


def dp_bits():
    size = lax.axis_size("dp")
    bits = []
    bit = 1
    while bit < size:
        bits.append(bit)
        bit *= 2
    return bits


def split_dp(block):
    bits = dp_bits()
    lead = block.shape[:-2]
    rows, cols = block.shape[-2:]
    return block.reshape(lead + (2,) * len(bits) + (rows // lax.axis_size("dp"), cols))


def scatter_bits(view, bits):
    for i, bit in enumerate(bits):
        keep, got = halve_bit(view, bit, view.ndim - 3)
        if i == len(bits) - 1:
            view = keep.astype(F32) + got.astype(F32)
        else:
            view = add(keep, got)
    return view


ROWS = 64
LANES = 256


def call(kernel, outs, meta, *args, scratch=()):
    vmem = pl.BlockSpec(memory_space=pltpu.VMEM)
    return pl.pallas_call(
        kernel,
        out_shape=[jax.ShapeDtypeStruct(shape, dtype) for shape, dtype in outs],
        in_specs=[pl.BlockSpec(memory_space=pltpu.SMEM)] + [vmem] * len(args),
        out_specs=[vmem] * len(outs),
        scratch_shapes=[pltpu.VMEM(shape, dtype) for shape, dtype in scratch],
    )(meta, *args)


def is_diag(meta):
    return meta[0] == meta[1]


def ordered(diag, mine, other):
    return jnp.concatenate([jnp.where(diag, mine, other), jnp.where(diag, other, mine)], axis=-1)


def block_of(diag, x, half):
    return jnp.where(diag, x[:, :half], x[:, half:])


def rows_of(ref_mine, ref_other, diag, i, base=0):
    part = slice(base + i * ROWS, base + (i + 1) * ROWS)
    return ordered(diag, ref_mine[part, :].astype(F32), ref_other[part, :].astype(F32))


def join(scratch, bit, mine, other):
    n = mine.shape[0]
    scratch[pl.ds(pl.multiple_of(bit * n, n), n), :] = mine[...]
    scratch[pl.ds(pl.multiple_of((1 - bit) * n, n), n), :] = other[...]


def column_sum(x):
    return jnp.sum(x, axis=0, keepdims=True)


def mod_kernel(meta, cond, cond_o, w_ada, bias8, own, away, silu):
    diag = is_diag(meta)
    half = cond.shape[1]
    mine = jnp.where(diag, cond[...].astype(F32), cond_o[...].astype(F32))
    act = narrowed(mine / (1.0 + jnp.exp(-mine)))
    silu[...] = act.astype(F32)
    part = dot(act, w_ada[...])
    first = meta[0] == 0
    near = jnp.where(first, part[0:1], part[1:2])
    far = jnp.where(first, part[1:2], part[0:1])
    for i in range(6):
        span = slice(i * half, (i + 1) * half)
        own[i : i + 1, :] = near[:, span] + bias8[i : i + 1, :]
        away[i : i + 1, :] = far[:, span]
    own[6:8, :] = bias8[6:8, :]
    away[6:8, :] = jnp.zeros((2, half), F32)


def attention_kernel(
    meta, tc_m, tc_o, own, got_col, got_row, got_cross, w_qkv, wq_m, wq_o, b_qv, w_proj, wp_f, wp_b,
    mod_ref, h1_ref, qkv_ref, lse_ref, att_ref, bp_ref, bpb_ref, wq2, wp_a,
):
    diag = is_diag(meta)
    join(wq2, meta[2], wq_m, wq_o)
    wp_a[...] = jnp.where(diag, w_proj[...], wp_f[...])
    half = tc_m.shape[1]
    seq = tc_m.shape[0] // 2
    mod = ordered(diag, own[...] + got_row[...], got_col[...] + got_cross[...])
    mod_ref[...] = mod
    shift, scale = mod[0:1], mod[1:2]
    for i in range(seq // ROWS):
        n1, _ = norm_rowwise(rows_of(tc_m, tc_o, diag, i))
        h1_ref[i * ROWS : (i + 1) * ROWS, :] = narrowed(n1 * (1.0 + scale) + shift)
    for j in range(3):
        span = slice(j * half, (j + 1) * half)
        part = dot(h1_ref[:, :half], w_qkv[:, span]) + dot(h1_ref[:, half:], wq2[:, span])
        if j == 0:
            part = part + b_qv[0:1, :]
        if j == 2:
            part = part + b_qv[1:2, :]
        qkv_ref[:, span] = narrowed(part)
    for h in range(half // HEAD_SIZE):
        q, k, v = (qkv_ref[:, j * half + h * HEAD_SIZE : j * half + (h + 1) * HEAD_SIZE] for j in range(3))
        scores = dot_nt(q, k) * (HEAD_SIZE ** (-0.5))
        top = jnp.max(scores, axis=-1, keepdims=True)
        grown = jnp.exp(scores - top)
        total = jnp.sum(grown, axis=-1, keepdims=True)
        lse_ref[:, h : h + 1] = top + jnp.log(total)
        probs = narrowed(grown * (1.0 / total))
        att_ref[:, h * HEAD_SIZE : (h + 1) * HEAD_SIZE] = narrowed(dot(probs, v))
    for j, w in enumerate((wp_a, wp_b)):
        span = slice(j * half, (j + 1) * half)
        part = dot(att_ref[...], w[...])
        bp_ref[:, span] = part
        bpb_ref[:, span] = narrowed(part)


def mlp_kernel(
    meta, tc_m, tc_o, mod_ref, bp, bp_got, b_fc1, w_fc1, w1_m, w1_o, w_fc2, w2_d, w2f_m, w2f_o, w2s_m, w2s_o,
    br1_ref, h2_ref, dbr_ref, act_ref, dup_ref, keep_ref, send_ref, dh_ref, dhb_ref, gb1_ref, w12, w2_a, w2_b,
):
    diag = is_diag(meta)
    join(w12, meta[2], w1_m, w1_o)

    @pl.when(diag)
    def _():
        w2_a[...] = w_fc2[...]
        w2_b[...] = w2_d[...]

    @pl.when(jnp.logical_not(diag))
    def _():
        join(w2_a, meta[2], w2f_m, w2f_o)
        join(w2_b, meta[3], w2s_m, w2s_o)

    half = tc_m.shape[1]
    seq = tc_m.shape[0] // 2
    mod = mod_ref[...]
    gate1, shift, scale, gate2, bias = mod[2:3], mod[3:4], mod[4:5], mod[5:6], mod[6:7]
    for i in range(seq // ROWS):
        part = slice(i * ROWS, (i + 1) * ROWS)
        branch = bp[part, :] + bp_got[part, :].astype(F32) + bias
        br1_ref[part, :] = branch
        mid = rows_of(tc_m, tc_o, diag, i) + gate1 * branch
        n2, _ = norm_rowwise(mid)
        h2_ref[part, :] = narrowed(n2 * (1.0 + scale) + shift)
        dbr_ref[part, :] = narrowed(rows_of(tc_m, tc_o, diag, i, seq) * gate2)
    for j in range(w_fc1.shape[1] // LANES):
        span = slice(j * LANES, (j + 1) * LANES)
        upper = dot(h2_ref[:, :half], w_fc1[:, span]) + dot(h2_ref[:, half:], w12[:, span]) + b_fc1[:, span]
        value, slope = gelu_pair(upper)
        act_ref[:, span] = narrowed(value)
        back = dot_nt(dbr_ref[:, :half], w2_a[span, :]) + dot_nt(dbr_ref[:, half:], w2_b[span, :])
        d_upper = back * slope
        gb1_ref[:, span] = column_sum(d_upper)
        dup_ref[:, span] = narrowed(d_upper)
    for j, w in enumerate((w_fc1, w12)):
        span = slice(j * half, (j + 1) * half)
        part = dot_nt(dup_ref[...], w[...])
        dh_ref[:, span] = part
        dhb_ref[:, span] = narrowed(part)
    down_a = dot(act_ref[...], w2_a[...])
    down_b = dot(act_ref[...], w2_b[...])
    keep_ref[...] = jnp.where(diag, down_a, down_b)
    send_ref[...] = narrowed(jnp.where(diag, down_b, down_a))


def output_kernel(meta, tc_m, mod_ref, br1, keep, got, b_fc2, out_ref, sum_ref):
    diag = is_diag(meta)
    half = tc_m.shape[1]
    gate1, gate2 = (block_of(diag, mod_ref[i : i + 1, :], half) for i in (2, 5))
    first = jnp.zeros((1, half), F32)
    second = jnp.zeros((1, half), F32)
    seq = tc_m.shape[0] // 2
    for i in range(seq // ROWS):
        part = slice(i * ROWS, (i + 1) * ROWS)
        mid = tc_m[part, :].astype(F32) + gate1 * block_of(diag, br1[part, :], half)
        branch = keep[part, :] + got[part, :].astype(F32) + b_fc2[...]
        out_ref[part, :] = narrowed(mid + gate2 * branch)
        g = tc_m[seq + i * ROWS : seq + (i + 1) * ROWS, :].astype(F32)
        first = first + column_sum(g * branch)
        second = second + column_sum(g * gate2)
    sum_ref[0:1, :] = first
    sum_ref[1:2, :] = second


def write_halves(bit, block, source, n, keep, send):
    for k in range(source.shape[0] // (2 * block)):
        part = slice(k * block, (k + 1) * block)
        keep[n, part, :] = source[pl.ds(pl.multiple_of((2 * k + bit) * block, block), block), :]
        send[n, part, :] = source[pl.ds(pl.multiple_of((2 * k + 1 - bit) * block, block), block), :]


def fc2_grad_kernel(block, meta, act, d_branch, *refs):
    half = d_branch.shape[1] // 2
    for n in range(2):
        part = narrowed(dot_tn(act[...], d_branch[:, n * half : (n + 1) * half]))
        if block:
            refs[2][...] = part
            write_halves(meta[2], block, refs[2], n, refs[0], refs[1])
        else:
            refs[0][n] = part


def fc1_grad_kernel(meta, hidden, d_upper, first, second):
    half = hidden.shape[1] // 2
    first[...] = narrowed(dot_tn(hidden[:, :half], d_upper[...]))
    second[...] = narrowed(dot_tn(hidden[:, half:], d_upper[...]))


def attention_grad_kernel(block, meta, hidden, d_qkv, att, d_branch, *refs):
    half = hidden.shape[1] // 2
    for n in range(2):
        span = slice(n * half, (n + 1) * half)
        qk = narrowed(dot_tn(hidden[:, span], d_qkv[:, : 2 * half]))
        v = narrowed(dot_tn(hidden[:, span], d_qkv[:, 2 * half :]))
        p = narrowed(dot_tn(att[...], d_branch[:, span]))
        if block:
            refs[4][...] = qk
            refs[5][:, :half] = v
            refs[5][:, half:] = p
            write_halves(meta[2], block, refs[4], n, refs[0], refs[1])
            write_halves(meta[2], block, refs[5], n, refs[2], refs[3])
        else:
            refs[0][n] = qk
            refs[1][n, :, :half] = v
            refs[1][n, :, half:] = p


def back_kernel(
    meta, tc_m, tc_o, mod_ref, br1, dh, dh_got, qkv, lse, w_proj, wp_f, wp_b, w_qkv, wq_m, wq_o,
    dmid_ref, dbr_ref, dqkv_ref, dh1_ref, dh1b_ref, wide_ref, bias_ref, datt_ref, wq2, wp_a,
):
    diag = is_diag(meta)
    join(wq2, meta[2], wq_m, wq_o)
    wp_a[...] = jnp.where(diag, w_proj[...], wp_f[...])
    half = tc_m.shape[1]
    seq = tc_m.shape[0] // 2
    mod = mod_ref[...]
    gate1, scale2 = mod[2:3], mod[4:5]
    sums = [jnp.zeros((1, 2 * half), F32) for _ in range(4)]
    for i in range(seq // ROWS):
        part = slice(i * ROWS, (i + 1) * ROWS)
        branch = br1[part, :]
        n2, rstd2 = norm_rowwise(rows_of(tc_m, tc_o, diag, i) + gate1 * branch)
        d_h2 = dh[part, :] + dh_got[part, :].astype(F32)
        d_mid = rows_of(tc_m, tc_o, diag, i, seq) + norm_backward(d_h2 * (1.0 + scale2), n2, rstd2)
        dmid_ref[part, :] = d_mid
        d_branch = d_mid * gate1
        dbr_ref[part, :] = narrowed(d_branch)
        for n, term in enumerate((d_mid * branch, d_h2, d_h2 * n2, d_branch)):
            sums[n] = sums[n] + column_sum(term)
    for n in range(4):
        wide_ref[n : n + 1, :] = sums[n]
    datt_ref[...] = narrowed(dot_nt(dbr_ref[:, :half], wp_a[...]) + dot_nt(dbr_ref[:, half:], wp_b[...]))
    root = HEAD_SIZE ** (-0.5)
    for h in range(half // HEAD_SIZE):
        q, k, v = (qkv[:, j * half + h * HEAD_SIZE : j * half + (h + 1) * HEAD_SIZE] for j in range(3))
        d_att = datt_ref[:, h * HEAD_SIZE : (h + 1) * HEAD_SIZE]
        probs = jnp.exp(dot_nt(q, k) * root - lse[:, h : h + 1])
        d_v = dot_tn(narrowed(probs), d_att)
        d_probs = dot_nt(d_att, v)
        d_scores = narrowed(probs * (d_probs - jnp.sum(probs * d_probs, axis=-1, keepdims=True)))
        d_q = dot(d_scores, k) * root
        d_k = dot_tn(d_scores, q) * root
        for j, term in enumerate((d_q, d_k, d_v)):
            dqkv_ref[:, j * half + h * HEAD_SIZE : j * half + (h + 1) * HEAD_SIZE] = narrowed(term)
        bias_ref[0:1, h * HEAD_SIZE : (h + 1) * HEAD_SIZE] = column_sum(d_q)
        bias_ref[1:2, h * HEAD_SIZE : (h + 1) * HEAD_SIZE] = column_sum(d_v)
    for j, w in enumerate((w_qkv, wq2)):
        span = slice(j * half, (j + 1) * half)
        part = dot_nt(dqkv_ref[...], w[...])
        dh1_ref[:, span] = part
        dh1b_ref[:, span] = narrowed(part)


def last_kernel(meta, tc_m, tc_o, mod_ref, d_mid, dh1, dh1_got, wide, bias, gb1, outs, silu, grad_ref, pay_ref):
    diag = is_diag(meta)
    half = tc_m.shape[1]
    scale1 = mod_ref[1:2, :]
    first = jnp.zeros((1, 2 * half), F32)
    second = jnp.zeros((1, 2 * half), F32)
    for i in range(tc_m.shape[0] // 2 // ROWS):
        part = slice(i * ROWS, (i + 1) * ROWS)
        n1, rstd1 = norm_rowwise(rows_of(tc_m, tc_o, diag, i))
        d_h1 = dh1[part, :] + dh1_got[part, :].astype(F32)
        grad = d_mid[part, :] + norm_backward(d_h1 * (1.0 + scale1), n1, rstd1)
        grad_ref[part, :] = narrowed(block_of(diag, grad, half))
        first = first + column_sum(d_h1)
        second = second + column_sum(d_h1 * n1)
    d_gate1, d_shift2, d_scale2, gb_proj = (block_of(diag, wide[n : n + 1, :], half) for n in range(4))
    first, second = (block_of(diag, term, half) for term in (first, second))
    roles = (first, second, d_gate1, d_shift2, d_scale2, outs[0:1, :], silu[0:1, :], silu[1:2, :])
    for n, term in enumerate(roles):
        pay_ref[0:1, n * half : (n + 1) * half] = term
    for n, term in enumerate((bias[0:1, :], bias[1:2, :], gb_proj, outs[1:2, :])):
        pay_ref[1:2, n * half : (n + 1) * half] = term
    pay_ref[1:2, 4 * half :] = gb1[...]


def finish_kernel(meta, own, got, w_ada, cond_ref, sum_ref, b_ada_ref, ada_ref):
    half = w_ada.shape[0]
    n = own.shape[0] - 1
    six = 6 * half
    first = meta[0] == 0
    sum_ref[...] = own[n : n + 1, :] + got[n : n + 1, :]
    near, far = own[:n, :six], got[:n, :six]
    b_ada_ref[...] = column_sum(near) + column_sum(far)
    pair = jnp.concatenate([jnp.where(first, near[:1], far[:1]), jnp.where(first, far[:1], near[:1])])
    cond_ref[...] = dot_nt(narrowed(pair), w_ada[...])
    rows = ada_ref.shape[0]
    spot = lax.broadcasted_iota(jnp.int32, (rows, half), 1) - lax.broadcasted_iota(jnp.int32, (rows, half), 0)
    select = narrowed(jnp.where(spot == meta[4] * rows, 1.0, 0.0))
    silu_0, silu_1 = narrowed(own[:n, six : six + half]), narrowed(own[:n, six + half : six + 2 * half])
    total = jnp.zeros(ada_ref.shape, F32)
    for values, silu in ((near, jnp.where(first, silu_0, silu_1)), (far, jnp.where(first, silu_1, silu_0))):
        total = total + dot(narrowed(dot_nt(select, silu)), narrowed(values))
    ada_ref[...] = total


def body(tokens, cond, w_ada, b_ada, w_qkv, b_qv, w_proj, b_proj, w_fc1, b_fc1, w_fc2, b_fc2, cotangent):
    r = lax.axis_index("row")
    c = lax.axis_index("col")
    diag = r == c
    d = lax.axis_index("dp")
    bits = dp_bits()
    bit_x, bit_z = bits[0], bits[min(1, len(bits) - 1)]
    bx, bz = (d // bit_x) % 2, (d // bit_z) % 2
    meta = jnp.stack([r, c, bx, bz, d]).astype(jnp.int32)
    half = tokens.shape[1]
    seq = tokens.shape[0] // 2
    hidden = w_fc1.shape[1]
    three = 3 * half

    def own_tokens(x):
        return lax.dynamic_slice_in_dim(x, r * seq, seq, 0)

    def both_rows(x):
        other = row_swap(x)
        return assembled(x, other)

    def assembled(x, other):
        return jnp.concatenate(
            [jnp.where(r == 0, x, other), jnp.where(r == 0, other, x)], axis=0
        )

    def half_rows(w, bit):
        n = w.shape[0] // 2
        return lax.dynamic_slice_in_dim(w, bit * n, n, 0)

    cond_other = col_swap(cond)
    tc_m = jnp.concatenate([own_tokens(tokens), own_tokens(cotangent)])
    tc_o = col_swap(tc_m)
    wp_b = lax.ppermute(w_proj, ("row", "col"), SECOND)
    wp_f = lax.ppermute(w_proj, ("row", "col"), FIRST)
    bias8 = jnp.concatenate([b_ada.reshape(6, half), b_proj[None], b_fc2[None]])

    own, away, silu_r = call(
        mod_kernel, [((8, half), F32), ((8, half), F32), ((2, half), F32)],
        meta, cond, cond_other, w_ada, bias8,
    )
    got_col = col_swap(own)
    got_row = row_swap(away)
    got_cross = cross_swap(away)
    wq_m = row_swap(half_rows(w_qkv, bx))
    w1_m = row_swap(half_rows(w_fc1, bx))
    w2_half = half_rows(w_fc2, bz)
    w2_half_x = half_rows(w_fc2, bx)
    w2s_m = lax.ppermute(w2_half, ("row", "col"), [(3, 1), (0, 2)])
    w2f_m = lax.ppermute(w2_half_x, ("row", "col"), FIRST)
    w2_d = lax.ppermute(w_fc2, ("row", "col"), [(1, 0), (2, 3)])
    wq_o = bit_swap(wq_m, bit_x)
    w1_o = bit_swap(w1_m, bit_x)
    w2s_o = off_diagonal_swap(w2s_m, bit_z)
    w2f_o = off_diagonal_swap(w2f_m, bit_x)
    mod, h1, qkv, lse, att, bp, bp_b = call(
        attention_kernel,
        [((8, 2 * half), F32), ((seq, 2 * half), BF16), ((seq, three), BF16), ((seq, 128), F32),
         ((seq, half), BF16), ((seq, 2 * half), F32), ((seq, 2 * half), BF16)],
        meta, tc_m, tc_o, own, got_col, got_row, got_cross, w_qkv, wq_m, wq_o, b_qv,
        w_proj, wp_f, wp_b, scratch=[(w_qkv.shape, BF16), (w_proj.shape, BF16)],
    )
    bp_got = col_swap(bp_b)
    br1, h2, d_br2, act, d_up, keep, send, dh2, dh2_b, gb1 = call(
        mlp_kernel,
        [((seq, 2 * half), F32), ((seq, 2 * half), BF16), ((seq, 2 * half), BF16), ((seq, hidden), BF16),
         ((seq, hidden), BF16), ((seq, half), F32), ((seq, half), BF16), ((seq, 2 * half), F32),
         ((seq, 2 * half), BF16), ((1, hidden), F32)],
        meta, tc_m, tc_o, mod, bp, bp_got, b_fc1[None], w_fc1, w1_m, w1_o, w_fc2,
        w2_d, w2f_m, w2f_o, w2s_m, w2s_o,
        scratch=[(w_fc1.shape, BF16), (w_fc2.shape, BF16), (w_fc2.shape, BF16)],
    )
    dh2_got = col_swap(dh2_b)
    down_got = col_swap(send)

    def whole_or_halves(rows, cols):
        block = rows // lax.axis_size("dp") * bit_x
        if block % 16:
            return 0, [((2, rows, cols), BF16)], ()
        return block, [((2, rows // 2, cols), BF16)] * 2, [((rows, cols), BF16)]

    block, outs_fc2, scratch = whole_or_halves(hidden, half)
    g_fc2 = call(functools.partial(fc2_grad_kernel, block), outs_fc2, meta, act, d_br2, scratch=scratch)
    g_fc1 = call(fc1_grad_kernel, [((half, hidden), BF16)] * 2, meta, h2, d_up)
    d_mid, d_br1, d_qkv, dh1, dh1_b, wide, bias, _ = call(
        back_kernel,
        [((seq, 2 * half), F32), ((seq, 2 * half), BF16), ((seq, three), BF16), ((seq, 2 * half), F32),
         ((seq, 2 * half), BF16), ((4, 2 * half), F32), ((2, half), F32), ((seq, half), BF16)],
        meta, tc_m, tc_o, mod, br1, dh2, dh2_got, qkv, lse, w_proj, wp_f, wp_b,
        w_qkv, wq_m, wq_o, scratch=[(w_qkv.shape, BF16), (w_proj.shape, BF16)],
    )
    dh1_got = col_swap(dh1_b)
    block, outs_qk, scratch = whole_or_halves(half, 2 * half)
    grads = call(
        functools.partial(attention_grad_kernel, block), outs_qk * 2,
        meta, h1, d_qkv, att, d_br1, scratch=list(scratch) * 2,
    )
    g_qk, g_vp = grads[: len(outs_qk)], grads[len(outs_qk) :]
    out_c, outs = call(
        output_kernel, [((seq, half), BF16), ((2, half), F32)],
        meta, tc_m, mod, br1, keep, down_got, b_fc2[None],
    )
    output = both_rows(out_c)
    tok_grad, pay = call(
        last_kernel, [((seq, half), BF16), ((2, 4 * half + hidden), F32)],
        meta, tc_m, tc_o, mod, d_mid, dh1, dh1_got, wide, bias, gb1, outs, silu_r,
    )
    token_gradient = both_rows(tok_grad)

    def by_column(first, second):
        got = row_swap(second)
        return add(first, got)

    def by_row(first, second):
        near = lax.ppermute(second, ("row", "col"), inverse(SECOND))
        far = lax.ppermute(first, ("row", "col"), inverse(FIRST))
        return add(near, jnp.where(diag, first, far))

    def over_x(pair, rows):
        if len(pair) == 1:
            view = split_dp(pair[0])
            view = add(*halve_bit(view, bits[0], view.ndim - 3))
        else:
            got = bit_swap(pair[1], bits[0])
            shape = (2,) * (len(bits) - 1) + (rows // lax.axis_size("dp"), got.shape[-1])
            view = [add(pair[0][n], got[n]).reshape(shape) for n in range(2)]
        return view[0], view[1]

    fc1 = split_dp(by_column(*g_fc1))
    fc1 = add(*halve_bit(fc1, bits[1], fc1.ndim - 4))
    fc1 = add(*halve_bit(fc1, bits[0], fc1.ndim - 3))
    out_fc1 = scatter_bits(fc1, bits[2:])[None]
    fc2 = by_row(*over_x(g_fc2, hidden))
    out_fc2 = scatter_bits(fc2, bits[1:])[None]
    qk = by_column(*over_x(g_qk, half))
    out_qk = scatter_bits(qk, bits[1:])
    vp = over_x(g_vp, half)
    v = by_column(vp[0][..., :half], vp[1][..., :half])
    p = by_row(vp[0][..., half:], vp[1][..., half:])
    vp = scatter_bits(jnp.concatenate([v, p], axis=-1), bits[1:])
    out_proj = vp[:, half:][None]
    out_qkv = jnp.concatenate([out_qk, vp[:, :half]], axis=-1)[None]

    for bit in bits[1:] + bits[:1]:
        got = bit_swap(pay, bit)
        pay = jnp.concatenate([pay[:-1], got[:-1], pay[-1:] + got[-1:]])
    got = row_swap(pay)
    d_cond, sums, out_b_ada, out_ada = call(
        finish_kernel,
        [((2, half), F32), ((1, 4 * half + hidden), F32), ((1, 6 * half), F32), ((half // lax.axis_size("dp"), 6 * half), F32)],
        meta, pay, got, w_ada,
    )
    out_b_ada, out_ada = out_b_ada[0], out_ada[None]
    d_cond = d_cond + col_swap(d_cond)
    d_cond = jnp.where(diag, d_cond, row_swap(d_cond))
    cond32 = cond.astype(F32)
    sig = jax.nn.sigmoid(cond32)
    grad_cond = narrowed(d_cond * sig * (1.0 + cond32 * (1.0 - sig)))
    out_b_qv = sums[:, : 2 * half].reshape(2, half)
    out_b_proj = sums[0, 2 * half : 3 * half]
    out_b_fc2 = sums[0, 3 * half : 4 * half]
    out_b_fc1 = sums[0, 4 * half :]
    return (
        output, token_gradient, grad_cond, out_ada, out_b_ada, out_qkv, out_b_qv,
        out_proj, out_b_proj, out_fc1, out_b_fc1, out_fc2, out_b_fc2,
    )


def solution(mesh):
    in_specs = (
        P("dp", "col"), P("dp", "col"), P("row", "col"), P("col"), P("row", "col"), P(None, "col"),
        P("row", "col"), P("col"), P("row", "col"), P("col"), P("row", "col"), P("col"), P("dp", "col"),
    )
    out_specs = (
        P("dp", "col"), P("dp", "col"), P("dp", "col"), P("row", "dp", "col"), P("col"),
        P("row", "dp", "col"), P(None, "col"), P("row", "dp", "col"), P("col"), P("row", "dp", "col"),
        P("col"), P("row", "dp", "col"), P("col"),
    )
    return jax.shard_map(body, mesh=mesh, in_specs=in_specs, out_specs=out_specs, check_vma=False)
```

```python
import functools

import jax
import jax.numpy as jnp
from jax import lax
from jax.experimental import pallas as pl
from jax.experimental.pallas import tpu as pltpu
from jax.sharding import PartitionSpec as P


HEAD_SIZE = 64
NORM_EPS = 1e-06
GELU_COEF = 0.7978845608028654
F32 = jnp.float32
BF16 = jnp.bfloat16


def narrowed(values):
    return values.astype(BF16)


def dot(a, b):
    return jnp.dot(a, b, preferred_element_type=F32)


def dot_nt(a, b):
    return lax.dot_general(a, b, (((1,), (1,)), ((), ())), preferred_element_type=F32)


def dot_tn(a, b):
    return lax.dot_general(a, b, (((0,), (0,)), ((), ())), preferred_element_type=F32)


def col_swap(x):
    return lax.ppermute(x, "col", [(0, 1), (1, 0)])


def row_swap(x):
    return lax.ppermute(x, "row", [(0, 1), (1, 0)])


def cross_swap(x):
    return lax.ppermute(x, ("row", "col"), [(0, 3), (1, 2), (2, 1), (3, 0)])


def bit_swap(x, bit):
    size = lax.axis_size("dp")
    return lax.ppermute(x, "dp", [(i, i ^ bit) for i in range(size)])


def off_diagonal_swap(x, bit):
    size = lax.axis_size("dp")
    pairs = [(4 * i + n, 4 * (i ^ bit) + n) for i in range(size) for n in (1, 2)]
    return lax.ppermute(x, ("dp", "row", "col"), pairs)


SECOND = [(1, 0), (2, 3), (3, 1), (0, 2)]
FIRST = [(2, 1), (1, 2)]


def inverse(pairs):
    return [(b, a) for a, b in pairs]


def gelu_pair(upper):
    inner = jnp.tanh(GELU_COEF * (upper + 0.044715 * upper * upper * upper))
    value = 0.5 * upper * (1.0 + inner)
    slope = 0.5 * (1.0 + inner) + 0.5 * upper * (1.0 - inner * inner) * GELU_COEF * (
        1.0 + 3.0 * 0.044715 * upper * upper
    )
    return value, slope


def norm_rowwise(values):
    mean = jnp.mean(values, axis=-1, keepdims=True)
    msq = jnp.mean(values * values, axis=-1, keepdims=True)
    rstd = lax.rsqrt(msq - mean * mean + NORM_EPS)
    return (values - mean) * rstd, rstd


def norm_backward(dnorm, normed, rstd):
    first = jnp.mean(dnorm, axis=-1, keepdims=True)
    second = jnp.mean(dnorm * normed, axis=-1, keepdims=True)
    return rstd * (dnorm - first - normed * second)


def halve_bit(block, bit, position):
    mine = (lax.axis_index("dp") // bit) % 2
    keep = lax.dynamic_index_in_dim(block, mine, position, keepdims=False)
    send = lax.dynamic_index_in_dim(block, 1 - mine, position, keepdims=False)
    got = bit_swap(send, bit)
    return keep, got


def add(a, b):
    return narrowed(a.astype(F32) + b.astype(F32))


def dp_bits():
    size = lax.axis_size("dp")
    bits = []
    bit = 1
    while bit < size:
        bits.append(bit)
        bit *= 2
    return bits


def split_dp(block):
    bits = dp_bits()
    lead = block.shape[:-2]
    rows, cols = block.shape[-2:]
    return block.reshape(lead + (2,) * len(bits) + (rows // lax.axis_size("dp"), cols))


def scatter_bits(view, bits):
    for i, bit in enumerate(bits):
        keep, got = halve_bit(view, bit, view.ndim - 3)
        if i == len(bits) - 1:
            view = keep.astype(F32) + got.astype(F32)
        else:
            view = add(keep, got)
    return view


ROWS = 64
LANES = 256


def call(kernel, outs, meta, *args, scratch=()):
    vmem = pl.BlockSpec(memory_space=pltpu.VMEM)
    return pl.pallas_call(
        kernel,
        out_shape=[jax.ShapeDtypeStruct(shape, dtype) for shape, dtype in outs],
        in_specs=[pl.BlockSpec(memory_space=pltpu.SMEM)] + [vmem] * len(args),
        out_specs=[vmem] * len(outs),
        scratch_shapes=[pltpu.VMEM(shape, dtype) for shape, dtype in scratch],
    )(meta, *args)


def is_diag(meta):
    return meta[0] == meta[1]


def ordered(diag, mine, other):
    return jnp.concatenate([jnp.where(diag, mine, other), jnp.where(diag, other, mine)], axis=-1)


def block_of(diag, x, half):
    return jnp.where(diag, x[:, :half], x[:, half:])


def rows_of(ref_mine, ref_other, diag, i, base=0):
    part = slice(base + i * ROWS, base + (i + 1) * ROWS)
    return ordered(diag, ref_mine[part, :].astype(F32), ref_other[part, :].astype(F32))


def join(scratch, bit, mine, other):
    n = mine.shape[0]
    scratch[pl.ds(pl.multiple_of(bit * n, n), n), :] = mine[...]
    scratch[pl.ds(pl.multiple_of((1 - bit) * n, n), n), :] = other[...]


def column_sum(x):
    return jnp.sum(x, axis=0, keepdims=True)


def mod_kernel(meta, cond, cond_o, w_ada, bias8, own, away, silu):
    diag = is_diag(meta)
    half = cond.shape[1]
    mine = jnp.where(diag, cond[...].astype(F32), cond_o[...].astype(F32))
    act = narrowed(mine / (1.0 + jnp.exp(-mine)))
    silu[...] = act.astype(F32)
    part = dot(act, w_ada[...])
    first = meta[0] == 0
    near = jnp.where(first, part[0:1], part[1:2])
    far = jnp.where(first, part[1:2], part[0:1])
    for i in range(6):
        span = slice(i * half, (i + 1) * half)
        own[i : i + 1, :] = near[:, span] + bias8[i : i + 1, :]
        away[i : i + 1, :] = far[:, span]
    own[6:8, :] = bias8[6:8, :]
    away[6:8, :] = jnp.zeros((2, half), F32)


def attention_kernel(
    meta, tc_m, tc_o, own, got_col, got_row, got_cross, w_qkv, wq_m, wq_o, b_qv, w_proj, wp_f, wp_b,
    mod_ref, h1_ref, qkv_ref, lse_ref, att_ref, bp_ref, bpb_ref, wq2, wp_a,
):
    diag = is_diag(meta)
    join(wq2, meta[2], wq_m, wq_o)
    wp_a[...] = jnp.where(diag, w_proj[...], wp_f[...])
    half = tc_m.shape[1]
    seq = tc_m.shape[0] // 2
    mod = ordered(diag, own[...] + got_row[...], got_col[...] + got_cross[...])
    mod_ref[...] = mod
    shift, scale = mod[0:1], mod[1:2]
    for i in range(seq // ROWS):
        n1, _ = norm_rowwise(rows_of(tc_m, tc_o, diag, i))
        h1_ref[i * ROWS : (i + 1) * ROWS, :] = narrowed(n1 * (1.0 + scale) + shift)
    for j in range(3):
        span = slice(j * half, (j + 1) * half)
        part = dot(h1_ref[:, :half], w_qkv[:, span]) + dot(h1_ref[:, half:], wq2[:, span])
        if j == 0:
            part = part + b_qv[0:1, :]
        if j == 2:
            part = part + b_qv[1:2, :]
        qkv_ref[:, span] = narrowed(part)
    for h in range(half // HEAD_SIZE):
        q, k, v = (qkv_ref[:, j * half + h * HEAD_SIZE : j * half + (h + 1) * HEAD_SIZE] for j in range(3))
        scores = dot_nt(q, k) * (HEAD_SIZE ** (-0.5))
        top = jnp.max(scores, axis=-1, keepdims=True)
        grown = jnp.exp(scores - top)
        total = jnp.sum(grown, axis=-1, keepdims=True)
        lse_ref[:, h : h + 1] = top + jnp.log(total)
        probs = narrowed(grown * (1.0 / total))
        att_ref[:, h * HEAD_SIZE : (h + 1) * HEAD_SIZE] = narrowed(dot(probs, v))
    for j, w in enumerate((wp_a, wp_b)):
        span = slice(j * half, (j + 1) * half)
        part = dot(att_ref[...], w[...])
        bp_ref[:, span] = part
        bpb_ref[:, span] = narrowed(part)


def mlp_kernel(
    meta, tc_m, tc_o, mod_ref, bp, bp_got, b_fc1, w_fc1, w1_m, w1_o, w1_n, w1_p, w_fc2, w2_d, w2f_m, w2f_o, w2s_m, w2s_o,
    br1_ref, h2_ref, dbr_ref, act_ref, dup_ref, keep_ref, send_ref, dh_ref, dhb_ref, gb1_ref, w12, w2_a, w2_b,
):
    diag = is_diag(meta)
    middle = w12.shape[1] // 2
    join(w12.at[:, :middle], meta[2], w1_m, w1_o)
    join(w12.at[:, middle:], meta[3], w1_n, w1_p)

    @pl.when(diag)
    def _():
        w2_a[...] = w_fc2[...]
        w2_b[...] = w2_d[...]

    @pl.when(jnp.logical_not(diag))
    def _():
        join(w2_a, meta[2], w2f_m, w2f_o)
        join(w2_b, meta[3], w2s_m, w2s_o)

    half = tc_m.shape[1]
    seq = tc_m.shape[0] // 2
    mod = mod_ref[...]
    gate1, shift, scale, gate2, bias = mod[2:3], mod[3:4], mod[4:5], mod[5:6], mod[6:7]
    for i in range(seq // ROWS):
        part = slice(i * ROWS, (i + 1) * ROWS)
        branch = bp[part, :] + bp_got[part, :].astype(F32) + bias
        br1_ref[part, :] = branch
        mid = rows_of(tc_m, tc_o, diag, i) + gate1 * branch
        n2, _ = norm_rowwise(mid)
        h2_ref[part, :] = narrowed(n2 * (1.0 + scale) + shift)
        dbr_ref[part, :] = narrowed(rows_of(tc_m, tc_o, diag, i, seq) * gate2)
    for j in range(w_fc1.shape[1] // LANES):
        span = slice(j * LANES, (j + 1) * LANES)
        upper = dot(h2_ref[:, :half], w_fc1[:, span]) + dot(h2_ref[:, half:], w12[:, span]) + b_fc1[:, span]
        value, slope = gelu_pair(upper)
        act_ref[:, span] = narrowed(value)
        back = dot_nt(dbr_ref[:, :half], w2_a[span, :]) + dot_nt(dbr_ref[:, half:], w2_b[span, :])
        d_upper = back * slope
        gb1_ref[:, span] = column_sum(d_upper)
        dup_ref[:, span] = narrowed(d_upper)
    for j, w in enumerate((w_fc1, w12)):
        span = slice(j * half, (j + 1) * half)
        part = dot_nt(dup_ref[...], w[...])
        dh_ref[:, span] = part
        dhb_ref[:, span] = narrowed(part)
    down_a = dot(act_ref[...], w2_a[...])
    down_b = dot(act_ref[...], w2_b[...])
    keep_ref[...] = jnp.where(diag, down_a, down_b)
    send_ref[...] = narrowed(jnp.where(diag, down_b, down_a))


def output_kernel(meta, tc_m, mod_ref, br1, keep, got, b_fc2, out_ref, sum_ref):
    diag = is_diag(meta)
    half = tc_m.shape[1]
    gate1, gate2 = (block_of(diag, mod_ref[i : i + 1, :], half) for i in (2, 5))
    first = jnp.zeros((1, half), F32)
    second = jnp.zeros((1, half), F32)
    seq = tc_m.shape[0] // 2
    for i in range(seq // ROWS):
        part = slice(i * ROWS, (i + 1) * ROWS)
        mid = tc_m[part, :].astype(F32) + gate1 * block_of(diag, br1[part, :], half)
        branch = keep[part, :] + got[part, :].astype(F32) + b_fc2[...]
        out_ref[part, :] = narrowed(mid + gate2 * branch)
        g = tc_m[seq + i * ROWS : seq + (i + 1) * ROWS, :].astype(F32)
        first = first + column_sum(g * branch)
        second = second + column_sum(g * gate2)
    sum_ref[0:1, :] = first
    sum_ref[1:2, :] = second


def write_halves(bit, block, source, n, keep, send):
    for k in range(source.shape[0] // (2 * block)):
        part = slice(k * block, (k + 1) * block)
        keep[n, part, :] = source[pl.ds(pl.multiple_of((2 * k + bit) * block, block), block), :]
        send[n, part, :] = source[pl.ds(pl.multiple_of((2 * k + 1 - bit) * block, block), block), :]


def fc2_grad_kernel(block, meta, act, d_branch, *refs):
    half = d_branch.shape[1] // 2
    for n in range(2):
        part = narrowed(dot_tn(act[...], d_branch[:, n * half : (n + 1) * half]))
        if block:
            refs[2][...] = part
            write_halves(meta[2], block, refs[2], n, refs[0], refs[1])
        else:
            refs[0][n] = part


def fc1_grad_kernel(meta, hidden, d_upper, first, second):
    half = hidden.shape[1] // 2
    first[...] = narrowed(dot_tn(hidden[:, :half], d_upper[...]))
    second[...] = narrowed(dot_tn(hidden[:, half:], d_upper[...]))


def attention_grad_kernel(block, meta, hidden, d_qkv, att, d_branch, *refs):
    half = hidden.shape[1] // 2
    for n in range(2):
        span = slice(n * half, (n + 1) * half)
        qk = narrowed(dot_tn(hidden[:, span], d_qkv[:, : 2 * half]))
        v = narrowed(dot_tn(hidden[:, span], d_qkv[:, 2 * half :]))
        p = narrowed(dot_tn(att[...], d_branch[:, span]))
        if block:
            refs[4][...] = qk
            refs[5][:, :half] = v
            refs[5][:, half:] = p
            write_halves(meta[2], block, refs[4], n, refs[0], refs[1])
            write_halves(meta[2], block, refs[5], n, refs[2], refs[3])
        else:
            refs[0][n] = qk
            refs[1][n, :, :half] = v
            refs[1][n, :, half:] = p


def back_kernel(
    meta, tc_m, tc_o, mod_ref, br1, dh, dh_got, qkv, lse, w_proj, wp_f, wp_b, w_qkv, wq_m, wq_o,
    dmid_ref, dbr_ref, dqkv_ref, dh1_ref, dh1b_ref, wide_ref, bias_ref, datt_ref, wq2, wp_a,
):
    diag = is_diag(meta)
    join(wq2, meta[2], wq_m, wq_o)
    wp_a[...] = jnp.where(diag, w_proj[...], wp_f[...])
    half = tc_m.shape[1]
    seq = tc_m.shape[0] // 2
    mod = mod_ref[...]
    gate1, scale2 = mod[2:3], mod[4:5]
    sums = [jnp.zeros((1, 2 * half), F32) for _ in range(4)]
    for i in range(seq // ROWS):
        part = slice(i * ROWS, (i + 1) * ROWS)
        branch = br1[part, :]
        n2, rstd2 = norm_rowwise(rows_of(tc_m, tc_o, diag, i) + gate1 * branch)
        d_h2 = dh[part, :] + dh_got[part, :].astype(F32)
        d_mid = rows_of(tc_m, tc_o, diag, i, seq) + norm_backward(d_h2 * (1.0 + scale2), n2, rstd2)
        dmid_ref[part, :] = d_mid
        d_branch = d_mid * gate1
        dbr_ref[part, :] = narrowed(d_branch)
        for n, term in enumerate((d_mid * branch, d_h2, d_h2 * n2, d_branch)):
            sums[n] = sums[n] + column_sum(term)
    for n in range(4):
        wide_ref[n : n + 1, :] = sums[n]
    datt_ref[...] = narrowed(dot_nt(dbr_ref[:, :half], wp_a[...]) + dot_nt(dbr_ref[:, half:], wp_b[...]))
    root = HEAD_SIZE ** (-0.5)
    for h in range(half // HEAD_SIZE):
        q, k, v = (qkv[:, j * half + h * HEAD_SIZE : j * half + (h + 1) * HEAD_SIZE] for j in range(3))
        d_att = datt_ref[:, h * HEAD_SIZE : (h + 1) * HEAD_SIZE]
        probs = jnp.exp(dot_nt(q, k) * root - lse[:, h : h + 1])
        d_v = dot_tn(narrowed(probs), d_att)
        d_probs = dot_nt(d_att, v)
        d_scores = narrowed(probs * (d_probs - jnp.sum(probs * d_probs, axis=-1, keepdims=True)))
        d_q = dot(d_scores, k) * root
        d_k = dot_tn(d_scores, q) * root
        for j, term in enumerate((d_q, d_k, d_v)):
            dqkv_ref[:, j * half + h * HEAD_SIZE : j * half + (h + 1) * HEAD_SIZE] = narrowed(term)
        bias_ref[0:1, h * HEAD_SIZE : (h + 1) * HEAD_SIZE] = column_sum(d_q)
        bias_ref[1:2, h * HEAD_SIZE : (h + 1) * HEAD_SIZE] = column_sum(d_v)
    for j, w in enumerate((w_qkv, wq2)):
        span = slice(j * half, (j + 1) * half)
        part = dot_nt(dqkv_ref[...], w[...])
        dh1_ref[:, span] = part
        dh1b_ref[:, span] = narrowed(part)


def last_kernel(meta, tc_m, tc_o, mod_ref, d_mid, dh1, dh1_got, wide, bias, gb1, outs, silu, grad_ref, pay_ref):
    diag = is_diag(meta)
    half = tc_m.shape[1]
    scale1 = mod_ref[1:2, :]
    first = jnp.zeros((1, 2 * half), F32)
    second = jnp.zeros((1, 2 * half), F32)
    for i in range(tc_m.shape[0] // 2 // ROWS):
        part = slice(i * ROWS, (i + 1) * ROWS)
        n1, rstd1 = norm_rowwise(rows_of(tc_m, tc_o, diag, i))
        d_h1 = dh1[part, :] + dh1_got[part, :].astype(F32)
        grad = d_mid[part, :] + norm_backward(d_h1 * (1.0 + scale1), n1, rstd1)
        grad_ref[part, :] = narrowed(block_of(diag, grad, half))
        first = first + column_sum(d_h1)
        second = second + column_sum(d_h1 * n1)
    d_gate1, d_shift2, d_scale2, gb_proj = (block_of(diag, wide[n : n + 1, :], half) for n in range(4))
    first, second = (block_of(diag, term, half) for term in (first, second))
    roles = (first, second, d_gate1, d_shift2, d_scale2, outs[0:1, :], silu[0:1, :], silu[1:2, :])
    for n, term in enumerate(roles):
        pay_ref[0:1, n * half : (n + 1) * half] = term
    for n, term in enumerate((bias[0:1, :], bias[1:2, :], gb_proj, outs[1:2, :])):
        pay_ref[1:2, n * half : (n + 1) * half] = term
    pay_ref[1:2, 4 * half :] = gb1[...]


def finish_kernel(meta, own, got, w_ada, cond_ref, sum_ref, b_ada_ref, ada_ref):
    half = w_ada.shape[0]
    n = own.shape[0] - 1
    six = 6 * half
    first = meta[0] == 0
    sum_ref[...] = own[n : n + 1, :] + got[n : n + 1, :]
    near, far = own[:n, :six], got[:n, :six]
    b_ada_ref[...] = column_sum(near) + column_sum(far)
    pair = jnp.concatenate([jnp.where(first, near[:1], far[:1]), jnp.where(first, far[:1], near[:1])])
    cond_ref[...] = dot_nt(narrowed(pair), w_ada[...])
    rows = ada_ref.shape[0]
    spot = lax.broadcasted_iota(jnp.int32, (rows, half), 1) - lax.broadcasted_iota(jnp.int32, (rows, half), 0)
    select = narrowed(jnp.where(spot == meta[4] * rows, 1.0, 0.0))
    silu_0, silu_1 = narrowed(own[:n, six : six + half]), narrowed(own[:n, six + half : six + 2 * half])
    total = jnp.zeros(ada_ref.shape, F32)
    for values, silu in ((near, jnp.where(first, silu_0, silu_1)), (far, jnp.where(first, silu_1, silu_0))):
        total = total + dot(narrowed(dot_nt(select, silu)), narrowed(values))
    ada_ref[...] = total


def body(tokens, cond, w_ada, b_ada, w_qkv, b_qv, w_proj, b_proj, w_fc1, b_fc1, w_fc2, b_fc2, cotangent):
    r = lax.axis_index("row")
    c = lax.axis_index("col")
    diag = r == c
    d = lax.axis_index("dp")
    bits = dp_bits()
    bit_x, bit_z = bits[0], bits[min(1, len(bits) - 1)]
    bx, bz = (d // bit_x) % 2, (d // bit_z) % 2
    meta = jnp.stack([r, c, bx, bz, d]).astype(jnp.int32)
    half = tokens.shape[1]
    seq = tokens.shape[0] // 2
    hidden = w_fc1.shape[1]
    three = 3 * half

    def own_tokens(x):
        return lax.dynamic_slice_in_dim(x, r * seq, seq, 0)

    def both_rows(x):
        other = row_swap(x)
        return assembled(x, other)

    def assembled(x, other):
        return jnp.concatenate(
            [jnp.where(r == 0, x, other), jnp.where(r == 0, other, x)], axis=0
        )

    def half_rows(w, bit):
        n = w.shape[0] // 2
        return lax.dynamic_slice_in_dim(w, bit * n, n, 0)

    cond_other = col_swap(cond)
    tc_m = jnp.concatenate([own_tokens(tokens), own_tokens(cotangent)])
    tc_o = col_swap(tc_m)
    wp_b = lax.ppermute(w_proj, ("row", "col"), SECOND)
    wp_f = lax.ppermute(w_proj, ("row", "col"), FIRST)
    bias8 = jnp.concatenate([b_ada.reshape(6, half), b_proj[None], b_fc2[None]])

    own, away, silu_r = call(
        mod_kernel, [((8, half), F32), ((8, half), F32), ((2, half), F32)],
        meta, cond, cond_other, w_ada, bias8,
    )
    got_col = col_swap(own)
    got_row = row_swap(away)
    got_cross = cross_swap(away)
    wq_m = row_swap(half_rows(w_qkv, bx))
    w2_half = half_rows(w_fc2, bz)
    w2_half_x = half_rows(w_fc2, bx)
    w2s_m = lax.ppermute(w2_half, ("row", "col"), [(3, 1), (0, 2)])
    w2f_m = lax.ppermute(w2_half_x, ("row", "col"), FIRST)
    w2_d = lax.ppermute(w_fc2, ("row", "col"), [(1, 0), (2, 3)])
    wq_o = bit_swap(wq_m, bit_x)
    wide = hidden // 2
    w1_m = row_swap(half_rows(w_fc1[:, :wide], bx))
    w1_n = row_swap(half_rows(w_fc1[:, wide:], bz))
    w1_o = bit_swap(w1_m, bit_x)
    w1_p = bit_swap(w1_n, bit_z)
    w2s_o = off_diagonal_swap(w2s_m, bit_z)
    w2f_o = off_diagonal_swap(w2f_m, bit_x)
    mod, h1, qkv, lse, att, bp, bp_b = call(
        attention_kernel,
        [((8, 2 * half), F32), ((seq, 2 * half), BF16), ((seq, three), BF16), ((seq, 128), F32),
         ((seq, half), BF16), ((seq, 2 * half), F32), ((seq, 2 * half), BF16)],
        meta, tc_m, tc_o, own, got_col, got_row, got_cross, w_qkv, wq_m, wq_o, b_qv,
        w_proj, wp_f, wp_b, scratch=[(w_qkv.shape, BF16), (w_proj.shape, BF16)],
    )
    bp_got = col_swap(bp_b)
    br1, h2, d_br2, act, d_up, keep, send, dh2, dh2_b, gb1 = call(
        mlp_kernel,
        [((seq, 2 * half), F32), ((seq, 2 * half), BF16), ((seq, 2 * half), BF16), ((seq, hidden), BF16),
         ((seq, hidden), BF16), ((seq, half), F32), ((seq, half), BF16), ((seq, 2 * half), F32),
         ((seq, 2 * half), BF16), ((1, hidden), F32)],
        meta, tc_m, tc_o, mod, bp, bp_got, b_fc1[None], w_fc1, w1_m, w1_o, w1_n, w1_p, w_fc2,
        w2_d, w2f_m, w2f_o, w2s_m, w2s_o,
        scratch=[(w_fc1.shape, BF16), (w_fc2.shape, BF16), (w_fc2.shape, BF16)],
    )
    dh2_got = col_swap(dh2_b)
    down_got = col_swap(send)

    def whole_or_halves(rows, cols):
        block = rows // lax.axis_size("dp") * bit_x
        if block % 16:
            return 0, [((2, rows, cols), BF16)], ()
        return block, [((2, rows // 2, cols), BF16)] * 2, [((rows, cols), BF16)]

    block, outs_fc2, scratch = whole_or_halves(hidden, half)
    g_fc2 = call(functools.partial(fc2_grad_kernel, block), outs_fc2, meta, act, d_br2, scratch=scratch)
    g_fc1 = call(fc1_grad_kernel, [((half, hidden), BF16)] * 2, meta, h2, d_up)
    d_mid, d_br1, d_qkv, dh1, dh1_b, wide, bias, _ = call(
        back_kernel,
        [((seq, 2 * half), F32), ((seq, 2 * half), BF16), ((seq, three), BF16), ((seq, 2 * half), F32),
         ((seq, 2 * half), BF16), ((4, 2 * half), F32), ((2, half), F32), ((seq, half), BF16)],
        meta, tc_m, tc_o, mod, br1, dh2, dh2_got, qkv, lse, w_proj, wp_f, wp_b,
        w_qkv, wq_m, wq_o, scratch=[(w_qkv.shape, BF16), (w_proj.shape, BF16)],
    )
    dh1_got = col_swap(dh1_b)
    block, outs_qk, scratch = whole_or_halves(half, 2 * half)
    grads = call(
        functools.partial(attention_grad_kernel, block), outs_qk * 2,
        meta, h1, d_qkv, att, d_br1, scratch=list(scratch) * 2,
    )
    g_qk, g_vp = grads[: len(outs_qk)], grads[len(outs_qk) :]
    out_c, outs = call(
        output_kernel, [((seq, half), BF16), ((2, half), F32)],
        meta, tc_m, mod, br1, keep, down_got, b_fc2[None],
    )
    output = both_rows(out_c)
    tok_grad, pay = call(
        last_kernel, [((seq, half), BF16), ((2, 4 * half + hidden), F32)],
        meta, tc_m, tc_o, mod, d_mid, dh1, dh1_got, wide, bias, gb1, outs, silu_r,
    )
    token_gradient = both_rows(tok_grad)

    def by_column(first, second):
        got = row_swap(second)
        return add(first, got)

    def by_row(first, second):
        near = lax.ppermute(second, ("row", "col"), inverse(SECOND))
        far = lax.ppermute(first, ("row", "col"), inverse(FIRST))
        return add(near, jnp.where(diag, first, far))

    def over_x(pair, rows):
        if len(pair) == 1:
            view = split_dp(pair[0])
            view = add(*halve_bit(view, bits[0], view.ndim - 3))
        else:
            got = bit_swap(pair[1], bits[0])
            shape = (2,) * (len(bits) - 1) + (rows // lax.axis_size("dp"), got.shape[-1])
            view = [add(pair[0][n], got[n]).reshape(shape) for n in range(2)]
        return view[0], view[1]

    fc1 = split_dp(by_column(*g_fc1))
    fc1 = add(*halve_bit(fc1, bits[1], fc1.ndim - 4))
    fc1 = add(*halve_bit(fc1, bits[0], fc1.ndim - 3))
    out_fc1 = scatter_bits(fc1, bits[2:])[None]
    fc2 = by_row(*over_x(g_fc2, hidden))
    out_fc2 = scatter_bits(fc2, bits[1:])[None]
    qk = by_column(*over_x(g_qk, half))
    out_qk = scatter_bits(qk, bits[1:])
    vp = over_x(g_vp, half)
    v = by_column(vp[0][..., :half], vp[1][..., :half])
    p = by_row(vp[0][..., half:], vp[1][..., half:])
    vp = scatter_bits(jnp.concatenate([v, p], axis=-1), bits[1:])
    out_proj = vp[:, half:][None]
    out_qkv = jnp.concatenate([out_qk, vp[:, :half]], axis=-1)[None]

    for bit in bits[1:] + bits[:1]:
        got = bit_swap(pay, bit)
        pay = jnp.concatenate([pay[:-1], got[:-1], pay[-1:] + got[-1:]])
    got = row_swap(pay)
    d_cond, sums, out_b_ada, out_ada = call(
        finish_kernel,
        [((2, half), F32), ((1, 4 * half + hidden), F32), ((1, 6 * half), F32), ((half // lax.axis_size("dp"), 6 * half), F32)],
        meta, pay, got, w_ada,
    )
    out_b_ada, out_ada = out_b_ada[0], out_ada[None]
    d_cond = d_cond + col_swap(d_cond)
    d_cond = jnp.where(diag, d_cond, row_swap(d_cond))
    cond32 = cond.astype(F32)
    sig = jax.nn.sigmoid(cond32)
    grad_cond = narrowed(d_cond * sig * (1.0 + cond32 * (1.0 - sig)))
    out_b_qv = sums[:, : 2 * half].reshape(2, half)
    out_b_proj = sums[0, 2 * half : 3 * half]
    out_b_fc2 = sums[0, 3 * half : 4 * half]
    out_b_fc1 = sums[0, 4 * half :]
    return (
        output, token_gradient, grad_cond, out_ada, out_b_ada, out_qkv, out_b_qv,
        out_proj, out_b_proj, out_fc1, out_b_fc1, out_fc2, out_b_fc2,
    )


def solution(mesh):
    in_specs = (
        P("dp", "col"), P("dp", "col"), P("row", "col"), P("col"), P("row", "col"), P(None, "col"),
        P("row", "col"), P("col"), P("row", "col"), P("col"), P("row", "col"), P("col"), P("dp", "col"),
    )
    out_specs = (
        P("dp", "col"), P("dp", "col"), P("dp", "col"), P("row", "dp", "col"), P("col"),
        P("row", "dp", "col"), P(None, "col"), P("row", "dp", "col"), P("col"), P("row", "dp", "col"),
        P("col"), P("row", "dp", "col"), P("col"),
    )
    return jax.shard_map(body, mesh=mesh, in_specs=in_specs, out_specs=out_specs, check_vma=False)
```
